256 devices in a mesh: mode: 16 (over y, z_lo, core), cell: 16 (over z_hi, x).
Axes of the slice: x: 4, y: 4, z: 8 (z_hi: 4, z_lo: 2; z = z_hi * 2 + z_lo), core: 2. Of those that a mesh axis runs over, the one named last changes fastest.
Arguments:
- adjoint: float32 [512, 36864], P('cell', 'mode'), may hold values from -6 to 6
- source: float32 [512, 36864], P('cell', 'mode'), may hold values from -6 to 6
- collision: bfloat16 [16, 16, 144, 36864], P(None, 'cell', None, 'mode'), may hold values from -0.018333333 to 1.0183333
- speed: float32 [36864], P('mode'), may hold values from 0.2 to 1
- direction: int32 [768], P('mode'), may hold values from 0 to 1
- labels: int32 [512], P('cell'), may hold values from 0 to 7
- conductance: float32 [8], replicated, may hold values from 0.3 to 1
Outputs:
- adjoint_out: float32 [512, 36864], P('cell', 'mode')
The draws below stay inside these ranges and needn't reach their ends.
All inputs are finite; a program needn't handle non-finite values.
Results may differ from the reference program's by a relative error of at most 0.005.
Values may be sent and summed in bfloat16 or wider, within the bound.
A program may use at most 64 MiB of HBM per device.

```python
import math
import jax
import jax.numpy as jnp
from jax import lax

BRANCH = 48
ITERS = 2
NMAT = 8
SUBW = 144
MODES = 36864
MBLK = 2304
QPTS = 768
CELLS = 512
N_MODE = 16
N_CELL = 16


def draw_collision(key, part):
    first, second = jax.random.split(jax.random.fold_in(key, 11), 2)
    spread = jax.random.normal(first, (MODES, MODES), jnp.float32)
    limit = 1.6 / math.sqrt(MODES)
    spread = jnp.clip(spread * (0.4 / math.sqrt(MODES)), -limit, limit)
    rates = jnp.exp(jax.random.uniform(second, (MODES,), jnp.float32, math.log(0.3), math.log(1.0)))
    diag_index = jnp.arange(MODES, dtype=jnp.int32)
    spread = spread.at[diag_index, diag_index].add(rates)
    return spread.reshape(MODES // MBLK, MBLK // SUBW, SUBW, MODES).astype(jnp.bfloat16)


def with_ends(entries, own_key, least, largest):
    shape = entries.shape
    spot = [jax.random.randint(jax.random.fold_in(own_key, axis), (), 0, shape[axis]) for axis in range(len(shape))]
    entries = entries.at[tuple(spot)].set(least)
    longest = shape.index(max(shape))
    spot[longest] = (spot[longest] + 1) % shape[longest]
    return entries.at[tuple(spot)].set(largest)


def block_scale(key, shape, cuts, smallest, high):
    gain, own = 1.0, jax.random.fold_in(key, 6)
    for position, parts in cuts:
        draws = jnp.exp(jax.random.uniform(jax.random.fold_in(own, position), (parts,), jnp.float32, smallest / len(cuts), high / len(cuts)))
        gain = gain * jnp.repeat(draws, shape[position] // parts).reshape([-1 if axis == position else 1 for axis in range(len(shape))])
    return gain


def noise(key, dims, scale, bound, cuts=(), kind=jnp.bfloat16):
    loudness = block_scale(key, dims, cuts, -0.22, 0.18) if cuts else 1.0
    result = jax.random.normal(key, dims, jnp.float32) * scale * loudness
    return jnp.minimum(jnp.maximum(result, -bound), bound).astype(kind)


def setup_inputs(seed: int = 0) -> dict:
    arg_keys = jax.random.split(jax.random.key(seed), 8)
    return {
        "adjoint": noise(arg_keys[0], (CELLS, MODES), 1.0, 6.0, ((0, 16), (1, 16)), jnp.float32),
        "source": noise(arg_keys[1], (CELLS, MODES), 1.0, 6.0, ((0, 16), (1, 16)), jnp.float32),
        "collision": draw_collision(jax.random.fold_in(arg_keys[7], 71), 0),
        "speed": jnp.clip(jnp.exp(math.log(1.0) - 1.609438 * jax.random.uniform(arg_keys[3], (MODES,), jnp.float32) ** block_scale(arg_keys[3], (MODES,), ((0, 16),), -0.2, 0.2)), 0.2, 1.0),
        "direction": with_ends(jax.random.randint(arg_keys[4], (QPTS,), 0, 2), jax.random.fold_in(arg_keys[4], 1), 0, 1).astype(jnp.int32),
        "labels": with_ends(jax.random.randint(arg_keys[5], (CELLS,), 0, NMAT), jax.random.fold_in(arg_keys[5], 1), 0, NMAT - 1).astype(jnp.int32),
        "conductance": jnp.clip(jax.random.uniform(arg_keys[6], (NMAT,), jnp.float32, 0.3, 1.0), 0.3, 1.0),
    }


relax_factor = 0.5


def material_scale(labels, conductance):
    matches = labels[:, None] == jnp.arange(conductance.shape[0], dtype=jnp.int32)[None, :]
    return jnp.sum(jnp.where(matches, conductance[None, :], 0.0), axis=1)


def upwind_pick(padded, sign_mode):
    return jnp.where(sign_mode[None, :] > 0, padded[2:], padded[:-2])


def reference(adjoint, source, collision, speed, direction, labels, conductance):
    conduct = material_scale(labels, conductance)
    sign_mode = jnp.repeat(2 * direction - 1, BRANCH)
    transport_rate = speed[None, :] * conduct[:, None]
    state = adjoint
    for sweep in range(ITERS):
        rounded = state.astype(jnp.bfloat16).reshape(CELLS, N_MODE, N_CELL, SUBW)

        def add_group(running, group):
            kernel_rows = lax.dynamic_index_in_dim(collision, group, 1, keepdims=False).reshape(N_MODE * SUBW, MODES)
            columns = lax.dynamic_index_in_dim(rounded, group, 2, keepdims=False).reshape(CELLS, N_MODE * SUBW)
            partial_value = jnp.dot(columns, kernel_rows, preferred_element_type=jnp.float32).astype(jnp.bfloat16)
            partial_value = lax.optimization_barrier(partial_value)
            return running + partial_value.astype(jnp.float32), None

        scattering, _ = lax.scan(add_group, jnp.zeros((CELLS, MODES), jnp.float32), jnp.arange(N_CELL, dtype=jnp.int32))
        padded = jnp.pad(state, ((1, 1), (0, 0)))
        transport = transport_rate * (state - upwind_pick(padded, sign_mode))
        state = state + relax_factor * (source - transport - scattering)
    return state
```

```python
import jax
import jax.numpy as jnp
from jax import lax
from jax.experimental import pallas as pl
from jax.experimental.pallas import tpu as pltpu
from jax.sharding import PartitionSpec as P

BRANCH = 48
RELAX = 0.5
MESH = pl.DeviceIdType.MESH
F32 = jnp.float32
BF16 = jnp.bfloat16

ROWS = 16
SUB = 144
WIDE = 2304
COLS = ((0, 1280), (1280, 1024))
TILE = 256

Z, YP0, YM0, YP1, YM1, FP0, FM0, FP1, FM1, CORE = 15, 16, 17, 18, 19, 20, 21, 22, 23, 24
RX, RZ, EDGE, SLOTS = 34, 46, 52, 54


def kernel(
    k_hbm, adj, src, speed, sign, kappa, out,
    kv, lam, base, sbuf, rbuf, xt, xm, pb, xrf, xrn, s32, zs, zrf, zrn, bsend, brecv,
    ssem, rsem, ksem,
):
    m, g = lax.axis_index("mode"), lax.axis_index("cell")
    y, low = m // 4, m % 4
    zl, core = low // 2, low % 2
    zh, x = g // 4, g % 4
    mate = y * 4 + zl * 2 + (1 - core)
    lowz = (1 - zl) * 2 + core
    zmate = y * 4 + lowz
    yp, ym, yf = (y + 1) % 4, (y + 3) % 4, (y + 2) % 4
    xp, xm1, xf = (x + 1) % 4, (x + 3) % 4, (x + 2) % 4
    zp, zm1, zf = (zh + 1) % 4, (zh + 3) % 4, (zh + 2) % 4
    at_yp, at_ym = {"mode": yp * 4 + low}, {"mode": ym * 4 + low}
    at_z, at_mate = {"mode": zmate}, {"mode": mate}
    at_xp, at_xm = {"cell": zh * 4 + xp}, {"cell": zh * 4 + xm1}
    at_zp, at_zm = {"cell": zp * 4 + x}, {"cell": zm1 * 4 + x}
    sent = {}

    def copy(u, slot, source, target, where):
        c = pltpu.make_async_remote_copy(
            src_ref=source, dst_ref=target, send_sem=ssem.at[u, slot], recv_sem=rsem.at[u, slot],
            device_id=where, device_id_type=MESH,
        )
        c.start()
        sent[u, slot] = c

    def got(u, slot):
        sent[u, slot].wait_recv()

    barrier = pltpu.get_barrier_semaphore()
    for d in range(1, 16):
        pl.semaphore_signal(barrier, inc=1, device_id={"cell": (g + d) % 16}, device_id_type=MESH)
    for where in (at_yp, at_ym, at_z, at_mate):
        pl.semaphore_signal(barrier, inc=1, device_id=where, device_id_type=MESH)
    kcopy = pltpu.make_async_copy(k_hbm, kv, ksem)
    kcopy.start()

    def pack(u):
        rows = pl.ds(ROWS * (u % 2), ROWS)
        state = adj if u < 2 else lam
        for q in range(16):
            start, off = (SUB * q) // 128 * 128, (SUB * q) % 128
            window = state[rows, start : start + 256]
            if off:
                window = pltpu.roll(window, 256 - off, axis=1)
            sbuf[u, q] = window.astype(BF16)

    place = x * 4 + zh

    def place_rows(p):
        return pl.ds(pl.multiple_of(p * ROWS, ROWS), ROWS)

    def a2a(u):
        for d in range(1, 16):
            to = (g + d) % 16
            copy(u, d - 1, sbuf.at[u, to], rbuf.at[u, place_rows(place)], {"cell": to})
        rbuf[u, place_rows(place), :] = sbuf[u, g]

    def blk(u, c):
        return xt.at[u, pl.ds(pl.multiple_of(c * SUB, 16), SUB), :]

    def half(u, c, h):
        return xt.at[u, pl.ds(pl.multiple_of(c * SUB, 16), SUB), pl.ds(128 * h, 128)]

    def own(u):
        for d in range(1, 16):
            got(u, d - 1)
        turned = rbuf[u].astype(F32).T
        xt[u, pl.ds(pl.multiple_of(m * SUB, 16), SUB), :] = turned[:SUB].astype(BF16)

    def to_mate(u, n, source):
        copy(u, CORE + n, source, source, at_mate)

    def gather(u, step):
        if step == 0:
            for slot, where in ((Z, at_z), (YP0, at_yp), (YM0, at_ym)):
                copy(u, slot, blk(u, m), blk(u, m), where)
            to_mate(u, 0, blk(u, m))
        elif step == 1:
            got(u, Z)
            for slot, where in ((YP1, at_yp), (YM1, at_ym)):
                copy(u, slot, blk(u, zmate), blk(u, zmate), where)
            to_mate(u, 1, blk(u, zmate))
        elif step in (2, 3):
            lo = low if step == 2 else lowz
            from_m, from_p = (YP0, YM0) if step == 2 else (YP1, YM1)
            fwd_p, fwd_m = (FP0, FM0) if step == 2 else (FP1, FM1)
            got(u, from_m)
            copy(u, fwd_p, half(u, ym * 4 + lo, 0), half(u, ym * 4 + lo, 0), at_yp)
            to_mate(u, 2 * step - 2, blk(u, ym * 4 + lo))
            got(u, from_p)
            copy(u, fwd_m, half(u, yp * 4 + lo, 1), half(u, yp * 4 + lo, 1), at_ym)
            to_mate(u, 2 * step - 1, blk(u, yp * 4 + lo))
        elif step in (4, 5):
            lo = low if step == 4 else lowz
            got(u, FP0 if step == 4 else FP1)
            to_mate(u, 2 * step - 2, half(u, yf * 4 + lo, 0))
            got(u, FM0 if step == 4 else FM1)
            to_mate(u, 2 * step - 1, half(u, yf * 4 + lo, 1))
        else:
            for n in range(10):
                got(u, CORE + n)

    def turn(u):
        @pl.loop(0, WIDE // TILE)
        def _(k):
            part = pl.ds(pl.multiple_of(k * TILE, TILE), TILE)
            xm[:, part] = xt[u, part, :].T

    def product(u, h):
        start, width = COLS[h]

        @pl.loop(0, width // TILE)
        def _(n):
            part = pl.ds(pl.multiple_of(start + n * TILE, TILE), TILE)
            pb[u, :, part] = jnp.dot(xm[...], kv[:, part], preferred_element_type=F32).astype(BF16)

    def cols(h):
        return pl.ds(COLS[h][0], COLS[h][1])

    def rx(to, upper):
        return pl.ds(pl.multiple_of(to * 64 + upper * 32, 32), 32)

    def rsx_start(u, h):
        s, c = RX + 6 * h, cols(h)
        copy(u, s, pb.at[u, rx(xf, 0), c], xrf.at[u, 0, :, c], at_xp)
        copy(u, s + 1, pb.at[u, rx(xf, 1), c], xrf.at[u, 1, :, c], at_xm)
        copy(u, s + 2, pb.at[u, rx(xp, 1), c], xrn.at[u, 0, pl.ds(32, 32), c], at_xp)
        copy(u, s + 3, pb.at[u, rx(xm1, 0), c], xrn.at[u, 1, pl.ds(0, 32), c], at_xm)

    def rsx_mid(u, h):
        s, c = RX + 6 * h, cols(h)
        got(u, s)
        r = rx(xp, 0)
        pb[u, r, c] = (pb[u, r, c].astype(F32) + xrf[u, 0, :, c].astype(F32)).astype(BF16)
        copy(u, s + 4, pb.at[u, r, c], xrn.at[u, 0, pl.ds(0, 32), c], at_xp)
        got(u, s + 1)
        r = rx(xm1, 1)
        pb[u, r, c] = (pb[u, r, c].astype(F32) + xrf[u, 1, :, c].astype(F32)).astype(BF16)
        copy(u, s + 5, pb.at[u, r, c], xrn.at[u, 1, pl.ds(32, 32), c], at_xm)

    def rz(to):
        return pl.ds(pl.multiple_of(to * ROWS, ROWS), ROWS)

    def rsx_fin(u, h):
        s, c = RX + 6 * h, cols(h)
        for slot in (2, 3, 4, 5):
            got(u, s + slot)
        r = pl.ds(pl.multiple_of(x * 64, 64), 64)
        total = pb[u, r, c].astype(F32) + xrn[u, 0, :, c].astype(F32) + xrn[u, 1, :, c].astype(F32)
        s32[u, :, c] = total
        zs[u, :, c] = total.astype(BF16)
        s = RZ + 3 * h
        if h == 0:
            copy(u, s, zs.at[u, rz(zf), c], zrf.at[u, :, c], at_zp)
            copy(u, s + 1, zs.at[u, rz(zm1), c], zrn.at[u, 1, :, c], at_zm)
        else:
            copy(u, s, zs.at[u, rz(zf), c], zrf.at[u, :, c], at_zm)
            copy(u, s + 1, zs.at[u, rz(zp), c], zrn.at[u, 0, :, c], at_zp)

    def rsz_mid(u, h):
        s, c = RZ + 3 * h, cols(h)
        got(u, s)
        r = rz(zp if h == 0 else zm1)
        zs[u, r, c] = (s32[u, r, c] + zrf[u, :, c].astype(F32)).astype(BF16)
        if h == 0:
            copy(u, s + 2, zs.at[u, r, c], zrn.at[u, 0, :, c], at_zp)
        else:
            copy(u, s + 2, zs.at[u, r, c], zrn.at[u, 1, :, c], at_zm)

    def finish(u, h):
        s, c = RZ + 3 * h, cols(h)
        got(u, s + 1)
        got(u, s + 2)
        total = s32[u, rz(zh), c] + zrn[u, 0, :, c].astype(F32) + zrn[u, 1, :, c].astype(F32)
        rows = pl.ds(ROWS * (u % 2), ROWS)
        new = base[u // 2, rows, c] - RELAX * total
        if u < 2:
            lam[rows, c] = new
        else:
            out[rows, c] = new

    def edge_send(it):
        state = adj if it == 0 else lam
        bsend[it, 0] = state[31:32, :]
        bsend[it, 1] = state[0:1, :]
        copy(2 * it, EDGE, bsend.at[it, 0], brecv.at[it, 0], {"cell": (g + 1) % 16})
        copy(2 * it, EDGE + 1, bsend.at[it, 1], brecv.at[it, 1], {"cell": (g + 15) % 16})

    def edge_use(it):
        state = adj if it == 0 else lam
        got(2 * it, EDGE)
        got(2 * it, EDGE + 1)
        first, last = g == 0, g == 15

        @pl.loop(0, WIDE // TILE)
        def _(n):
            c = pl.ds(pl.multiple_of(n * TILE, TILE), TILE)
            now = state[:, c]
            row = lax.broadcasted_iota(jnp.int32, now.shape, 0)
            before = jnp.where(first, 0.0, brecv[it, 0, :, c])
            after = jnp.where(last, 0.0, brecv[it, 1, :, c])
            down = jnp.where(row == 0, before, pltpu.roll(now, 1, axis=0))
            up = jnp.where(row == 31, after, pltpu.roll(now, 31, axis=0))
            pick = jnp.where(sign[:, c] > 0, up, down)
            transport = speed[:, c] * kappa[...] * (now - pick)
            base[it, :, c] = now + RELAX * (src[:, c] - transport)

    def gathers(u, *steps):
        for step in steps:
            gather(u, step)

    pack(0)
    pack(1)
    pl.semaphore_wait(barrier, 19)
    a2a(0)
    a2a(1)
    edge_send(0)
    own(0)
    gather(0, 0)
    own(1)
    gather(1, 0)
    edge_use(0)
    gathers(0, 1, 2, 3)
    gather(1, 1)
    gathers(0, 4, 5)
    gather(1, 2)
    gather(0, 6)
    kcopy.wait()
    turn(0)
    product(0, 0)
    rsx_start(0, 0)
    gather(1, 3)
    product(0, 1)
    rsx_start(0, 1)
    gathers(1, 4, 5)
    rsx_mid(0, 0)
    rsx_mid(0, 1)
    gather(1, 6)
    turn(1)
    product(1, 0)
    rsx_start(1, 0)
    product(1, 1)
    rsx_start(1, 1)
    rsx_fin(0, 0)
    rsx_fin(0, 1)
    rsz_mid(0, 0)
    rsz_mid(0, 1)
    rsx_mid(1, 0)
    rsx_mid(1, 1)
    finish(0, 0)
    finish(0, 1)
    pack(2)
    a2a(2)
    rsx_fin(1, 0)
    own(2)
    gather(2, 0)
    rsx_fin(1, 1)
    gathers(2, 1)
    rsz_mid(1, 0)
    gathers(2, 2)
    rsz_mid(1, 1)
    gathers(2, 3)
    finish(1, 0)
    finish(1, 1)
    pack(3)
    a2a(3)
    edge_send(1)
    gathers(2, 4, 5, 6)
    turn(2)
    product(2, 0)
    rsx_start(2, 0)
    own(3)
    gather(3, 0)
    product(2, 1)
    rsx_start(2, 1)
    gathers(3, 1)
    edge_use(1)
    rsx_mid(2, 0)
    gathers(3, 2)
    rsx_mid(2, 1)
    gathers(3, 3, 4, 5, 6)
    turn(3)
    product(3, 0)
    rsx_start(3, 0)
    product(3, 1)
    rsx_start(3, 1)
    rsx_fin(2, 0)
    rsx_fin(2, 1)
    rsz_mid(2, 0)
    rsz_mid(2, 1)
    rsx_mid(3, 0)
    rsx_mid(3, 1)
    finish(2, 0)
    finish(2, 1)
    rsx_fin(3, 0)
    rsx_fin(3, 1)
    rsz_mid(3, 0)
    rsz_mid(3, 1)
    finish(3, 0)
    finish(3, 1)
    for c in sent.values():
        c.wait_send()


def shards(adjoint, source, collision, speed, direction, labels, conductance):
    rows, width = adjoint.shape
    table = collision.reshape(-1, width)
    sign = jnp.broadcast_to((2 * direction - 1)[:, None], (direction.shape[0], BRANCH)).reshape(1, -1)
    matches = labels[:, None] == jnp.arange(conductance.shape[0], dtype=jnp.int32)[None, :]
    kappa = jnp.sum(jnp.where(matches, conductance[None, :], 0.0), axis=1, keepdims=True)
    vmem = pl.BlockSpec(memory_space=pltpu.VMEM)
    return pl.pallas_call(
        kernel,
        out_shape=jax.ShapeDtypeStruct((rows, width), F32),
        in_specs=[pl.BlockSpec(memory_space=pl.ANY)] + [vmem] * 5,
        out_specs=vmem,
        scratch_shapes=[
            pltpu.VMEM((WIDE, WIDE), BF16),
            pltpu.VMEM((32, WIDE), F32),
            pltpu.VMEM((2, 32, WIDE), F32),
            pltpu.VMEM((4, 16, ROWS, 256), BF16),
            pltpu.VMEM((4, 256, 256), BF16),
            pltpu.VMEM((4, WIDE, 256), BF16),
            pltpu.VMEM((256, WIDE), BF16),
            pltpu.VMEM((4, 256, WIDE), BF16),
            pltpu.VMEM((4, 2, 32, WIDE), BF16),
            pltpu.VMEM((4, 2, 64, WIDE), BF16),
            pltpu.VMEM((4, 64, WIDE), F32),
            pltpu.VMEM((4, 64, WIDE), BF16),
            pltpu.VMEM((4, ROWS, WIDE), BF16),
            pltpu.VMEM((4, 2, ROWS, WIDE), BF16),
            pltpu.VMEM((2, 2, 1, WIDE), F32),
            pltpu.VMEM((2, 2, 1, WIDE), F32),
            pltpu.SemaphoreType.DMA((4, SLOTS)),
            pltpu.SemaphoreType.DMA((4, SLOTS)),
            pltpu.SemaphoreType.DMA,
        ],
        compiler_params=pltpu.CompilerParams(collective_id=0, has_side_effects=True, vmem_limit_bytes=60 << 20),
    )(table, adjoint, source, speed[None, :], sign, kappa)


def solution(mesh):
    in_specs = (
        P("cell", "mode"),
        P("cell", "mode"),
        P(None, "cell", None, "mode"),
        P("mode"),
        P("mode"),
        P("cell"),
        P(),
    )
    return jax.shard_map(shards, mesh=mesh, in_specs=in_specs, out_specs=P("cell", "mode"), check_vma=False)
```

```python
import jax
import jax.numpy as jnp
from jax import lax
from jax.experimental import pallas as pl
from jax.experimental.pallas import tpu as pltpu
from jax.sharding import PartitionSpec as P

BRANCH = 48
RELAX = 0.5
MESH = pl.DeviceIdType.MESH
F32 = jnp.float32
BF16 = jnp.bfloat16

ROWS = 16
SUB = 144
WIDE = 2304
COLS = ((0, 1280), (1280, 1024))
TILE = 256

ALL, Z, P0, M0, P1, M1, F0, F1, CORE, RX, RZ, EDGE, THERE, BACK, RECV = 0, 1, 3, 5, 7, 9, 11, 12, 13, 14, 20, 24, 25, 26, 27
SALL, SGATHER, SX, SZ, SEDGE, STHERE, SBACK, SEND = 0, 1, 2, 3, 4, 5, 6, 7


def kernel(
    k_hbm, adj_hbm, src_hbm, speed, direction, labels, conductance, out,
    adj, src, sign, kappa, kv, kt, lam, base, sbuf, rbuf, tbuf, trecv, base_t, wbuf, wrecv, xt, xm,
    pt, xrft, xrnt, s32t, zst, zrft, zrnt,
    pb, xrf, xrn, s32, zs, zrf, zrn, bsend, brecv,
    ssem, rsem, insem,
):
    m, g = lax.axis_index("mode"), lax.axis_index("cell")
    y, low = m // 4, m % 4
    zl, core = low // 2, low % 2
    zh, x = g // 4, g % 4
    mate = y * 4 + zl * 2 + (1 - core)
    lowz = (1 - zl) * 2 + core
    zmate = y * 4 + lowz
    yp, ym, yf = (y + 1) % 4, (y + 3) % 4, (y + 2) % 4
    xp, xm1, xf = (x + 1) % 4, (x + 3) % 4, (x + 2) % 4
    zp, zm1, zf = (zh + 1) % 4, (zh + 3) % 4, (zh + 2) % 4
    at_yp, at_ym = {"mode": yp * 4 + low}, {"mode": ym * 4 + low}
    at_z, at_mate = {"mode": zmate}, {"mode": mate}
    at_xp, at_xm = {"cell": zh * 4 + xp}, {"cell": zh * 4 + xm1}
    at_zp, at_zm = {"cell": zp * 4 + x}, {"cell": zm1 * 4 + x}

    def copy(u, send, recv, source, target, where):
        pltpu.make_async_remote_copy(
            src_ref=source, dst_ref=target, send_sem=ssem.at[u, send], recv_sem=rsem.at[u, recv],
            device_id=where, device_id_type=MESH,
        ).start()

    def got(u, recv, like):
        pltpu.make_async_copy(like, like, rsem.at[u, recv]).wait()

    def gone(u, send, like):
        pltpu.make_async_copy(like, like, ssem.at[u, send]).wait()

    barrier = pltpu.get_barrier_semaphore()
    for d in range(1, 16):
        pl.semaphore_signal(barrier, inc=1, device_id={"cell": (g + d) % 16}, device_id_type=MESH)
    for where in (at_yp, at_ym, at_z, at_mate):
        pl.semaphore_signal(barrier, inc=1, device_id=where, device_id_type=MESH)
    incopies = [
        pltpu.make_async_copy(a, b, insem.at[n]) for n, (a, b) in enumerate(((adj_hbm, adj), (src_hbm, src), (k_hbm, kv)))
    ]
    for c in incopies:
        c.start()

    def prepare():
        lane = lax.broadcasted_iota(jnp.int32, (1, 128), 1)
        for t in range(WIDE // 128):
            first = t * 128 // BRANCH
            v = jnp.full((1, 128), direction[first], jnp.int32)
            for q in range(first + 1, (t * 128 + 127) // BRANCH + 1):
                v = jnp.where(lane >= q * BRANCH - t * 128, direction[q], v)
            sign[:, t * 128 : t * 128 + 128] = 2 * v - 1
        row = lax.broadcasted_iota(jnp.int32, (32, 128), 0)
        k = jnp.zeros((32, 128), F32)
        for r in range(32):
            k = jnp.where(row == r, conductance[labels[r]], k)
        kappa[...] = k

    place = x * 4 + zh

    def place_rows(p):
        return pl.ds(pl.multiple_of(p * ROWS, ROWS), ROWS)

    def window(q):
        return (SUB * q) // 128 * 128, (SUB * q) % 128

    def pack(u, state, into):
        rows = pl.ds(ROWS * u, ROWS)
        for q in range(16):
            start, off = window(q)
            part = state[rows, start : start + 256]
            if off:
                part = pltpu.roll(part, 256 - off, axis=1)
            into[u, q] = part.astype(BF16)

    def exchange(u, send, recv, source, target):
        for d in range(1, 16):
            to = (g + d) % 16
            copy(u, send, recv, source.at[u, to], target.at[u, place_rows(place)], {"cell": to})
        target[u, place_rows(place), :] = source[u, g]

    def pack_state(u):
        pack(u, adj, sbuf)

    def pack_base(u):
        pack(u, base.at[0], tbuf)

    def a2a(u):
        exchange(u, SALL, ALL, sbuf, rbuf)

    def there(u):
        exchange(u, STHERE, THERE, tbuf, trecv)

    def there_use(u):
        got(u, THERE, trecv.at[u, pl.ds(0, 15 * ROWS)])
        base_t[u] = trecv[u].astype(F32).T[:SUB]

    def flip(*strips):
        for j in strips:
            @pl.loop(0, WIDE // TILE)
            def _(i):
                part = pl.ds(pl.multiple_of(i * TILE, TILE), TILE)
                kt[j * TILE : (j + 1) * TILE, part] = kv[part, j * TILE : (j + 1) * TILE].T

    def blk(u, c):
        return xt.at[u, pl.ds(pl.multiple_of(c * SUB, 16), SUB), :]

    def half(u, c, h):
        return xt.at[u, pl.ds(pl.multiple_of(c * SUB, 16), SUB), pl.ds(128 * h, 128)]

    def own(u):
        got(u, ALL, rbuf.at[u, pl.ds(0, 15 * ROWS)])
        turned = rbuf[u].astype(F32).T
        xt[u, pl.ds(pl.multiple_of(m * SUB, 16), SUB), :] = turned[:SUB].astype(BF16)

    def to_mate(u, c):
        copy(u, SGATHER, CORE, blk(u, c), blk(u, c), at_mate)

    def gather(u, step):
        one, part = xt.at[u, pl.ds(0, SUB), :], xt.at[u, pl.ds(0, SUB), pl.ds(0, 128)]
        if step == 0:
            for slot, h, where in ((Z, 0, at_z), (P0, 0, at_yp), (M0, 1, at_ym), (Z, 1, at_z), (P0, 1, at_yp), (M0, 0, at_ym)):
                copy(u, SGATHER, slot + h, half(u, m, h), half(u, m, h), where)
            to_mate(u, m)
        elif step == 1:
            got(u, Z, part)
            copy(u, SGATHER, P1, half(u, zmate, 0), half(u, zmate, 0), at_yp)
            got(u, Z + 1, part)
            copy(u, SGATHER, M1 + 1, half(u, zmate, 1), half(u, zmate, 1), at_ym)
            copy(u, SGATHER, P1 + 1, half(u, zmate, 1), half(u, zmate, 1), at_yp)
            copy(u, SGATHER, M1, half(u, zmate, 0), half(u, zmate, 0), at_ym)
            to_mate(u, zmate)
        elif step in (2, 3):
            lo = low if step == 2 else lowz
            p, n, far = (P0, M0, F0) if step == 2 else (P1, M1, F1)
            got(u, p, part)
            copy(u, SGATHER, far, half(u, ym * 4 + lo, 0), half(u, ym * 4 + lo, 0), at_yp)
            got(u, n + 1, part)
            copy(u, SGATHER, far, half(u, yp * 4 + lo, 1), half(u, yp * 4 + lo, 1), at_ym)
            got(u, p + 1, part)
            to_mate(u, ym * 4 + lo)
            got(u, n, part)
            to_mate(u, yp * 4 + lo)
        elif step in (4, 5):
            got(u, F0 if step == 4 else F1, one)
            to_mate(u, yf * 4 + (low if step == 4 else lowz))
        else:
            got(u, CORE, xt.at[u, pl.ds(0, 8 * SUB), :])

    def turn(u):
        @pl.loop(0, WIDE // TILE)
        def _(k):
            part = pl.ds(pl.multiple_of(k * TILE, TILE), TILE)
            xm[:, part] = xt[u, part, :].T

    def product(u, h):
        start, width = COLS[h]

        @pl.loop(0, width // TILE)
        def _(n):
            part = pl.ds(pl.multiple_of(start + n * TILE, TILE), TILE)
            pb[u - 2, :, part] = jnp.dot(xm[...], kv[:, part], preferred_element_type=F32).astype(BF16)

    def tproduct(u, p):
        for z in (2 * p, 2 * p + 1):
            rows = kt[z * 4 * SUB : (z + 1) * 4 * SUB, :]
            pt[u, z] = jnp.dot(rows, xt[u], preferred_element_type=F32).astype(BF16).reshape(4, SUB, 256)

    def trsx_start(u, p):
        zz = pl.ds(2 * p, 2)
        if p == 0:
            copy(u, SX, RX, pt.at[u, zz, xf], xrft.at[u, 0], at_xp)
            copy(u, SX, RX + 2, pt.at[u, zz, xm1], xrnt.at[u, 1, zz], at_xm)
        else:
            copy(u, SX, RX + 1, pt.at[u, zz, xf], xrft.at[u, 1], at_xm)
            copy(u, SX, RX + 2, pt.at[u, zz, xp], xrnt.at[u, 0, zz], at_xp)

    def trsx_mid(u, p):
        zz, to, where = pl.ds(2 * p, 2), xp if p == 0 else xm1, at_xp if p == 0 else at_xm
        got(u, RX + p, xrft.at[u, p])
        pt[u, zz, to] = (pt[u, zz, to].astype(F32) + xrft[u, p].astype(F32)).astype(BF16)
        copy(u, SX, RX + 2, pt.at[u, zz, to], xrnt.at[u, p, zz], where)

    def trsx_fin(u):
        got(u, RX + 2, xrnt.at[u])
        for z in range(4):
            total = pt[u, z, x].astype(F32) + xrnt[u, 0, z].astype(F32) + xrnt[u, 1, z].astype(F32)
            s32t[u, z] = total
            zst[u, z] = total.astype(BF16)
        lo, hi = pl.ds(0, 128), pl.ds(128, 128)
        copy(u, SZ, RZ, zst.at[u, zf, :, lo], zrft.at[u, :, lo], at_zp)
        copy(u, SZ, RZ + 1, zst.at[u, zf, :, hi], zrft.at[u, :, hi], at_zm)
        copy(u, SZ, RZ + 2, zst.at[u, zm1, :, lo], zrnt.at[u, 1, :, lo], at_zm)
        copy(u, SZ, RZ + 2, zst.at[u, zp, :, hi], zrnt.at[u, 0, :, hi], at_zp)

    def trsz_mid(u, p):
        c, to, where = pl.ds(128 * p, 128), zp if p == 0 else zm1, at_zp if p == 0 else at_zm
        got(u, RZ + p, zrft.at[u, :, c])
        zst[u, to, :, c] = (s32t[u, to, :, c] + zrft[u, :, c].astype(F32)).astype(BF16)
        copy(u, SZ, RZ + 2, zst.at[u, to, :, c], zrnt.at[u, p, :, c], where)

    def tfinish(u):
        got(u, RZ + 2, zrnt.at[u])
        total = s32t[u, zh] + zrnt[u, 0].astype(F32) + zrnt[u, 1].astype(F32)
        new = base_t[u] - RELAX * total
        xt[u + 2, pl.ds(pl.multiple_of(m * SUB, 16), SUB), :] = new.astype(BF16)
        s32t[u, zh] = total

    def back(u):
        total = jnp.concatenate([s32t[u, zh], jnp.zeros((256 - SUB, 256), F32)], axis=0)
        wbuf[u] = total.T.astype(BF16)
        for d in range(1, 16):
            to = (g + d) % 16
            copy(u, SBACK, BACK, wbuf.at[u, place_rows(to % 4 * 4 + to // 4)], wrecv.at[u, g], {"cell": to})
        wrecv[u, g] = wbuf[u, place_rows(place), :]

    def back_use(u):
        got(u, BACK, wrecv.at[u, pl.ds(0, 15)])
        rows = pl.ds(ROWS * u, ROWS)
        lam[rows, :] = base[0, rows, :]
        for q in range(16):
            start, off = window(q)
            part = wrecv[u, q].astype(F32)
            if off:
                part = pltpu.roll(part, off, axis=1)
            lam[rows, start : start + 256] = lam[rows, start : start + 256] - RELAX * part

    def cols(h):
        return pl.ds(COLS[h][0], COLS[h][1])

    def rx(to, upper):
        return pl.ds(pl.multiple_of(to * 64 + upper * 32, 32), 32)

    def rsx_start(u, h):
        v = u - 2
        s, c = RX + 3 * h, cols(h)
        copy(u, SX, s, pb.at[v, rx(xf, 0), c], xrf.at[v, 0, :, c], at_xp)
        copy(u, SX, s + 1, pb.at[v, rx(xf, 1), c], xrf.at[v, 1, :, c], at_xm)
        copy(u, SX, s + 2, pb.at[v, rx(xp, 1), c], xrn.at[v, 0, pl.ds(32, 32), c], at_xp)
        copy(u, SX, s + 2, pb.at[v, rx(xm1, 0), c], xrn.at[v, 1, pl.ds(0, 32), c], at_xm)

    def rsx_mid(u, h):
        v = u - 2
        s, c = RX + 3 * h, cols(h)
        got(u, s, xrf.at[v, 0, :, c])
        r = rx(xp, 0)
        pb[v, r, c] = (pb[v, r, c].astype(F32) + xrf[v, 0, :, c].astype(F32)).astype(BF16)
        copy(u, SX, s + 2, pb.at[v, r, c], xrn.at[v, 0, pl.ds(0, 32), c], at_xp)
        got(u, s + 1, xrf.at[v, 1, :, c])
        r = rx(xm1, 1)
        pb[v, r, c] = (pb[v, r, c].astype(F32) + xrf[v, 1, :, c].astype(F32)).astype(BF16)
        copy(u, SX, s + 2, pb.at[v, r, c], xrn.at[v, 1, pl.ds(32, 32), c], at_xm)

    def rz(to):
        return pl.ds(pl.multiple_of(to * ROWS, ROWS), ROWS)

    def rsx_fin(u, h):
        v = u - 2
        c = cols(h)
        got(u, RX + 3 * h + 2, pb.at[v, pl.ds(0, 128), c])
        r = pl.ds(pl.multiple_of(x * 64, 64), 64)
        total = pb[v, r, c].astype(F32) + xrn[v, 0, :, c].astype(F32) + xrn[v, 1, :, c].astype(F32)
        s32[v, :, c] = total
        zs[v, :, c] = total.astype(BF16)
        s = RZ + 2 * h
        if h == 0:
            copy(u, SZ, s, zs.at[v, rz(zf), c], zrf.at[v, :, c], at_zp)
            copy(u, SZ, s + 1, zs.at[v, rz(zm1), c], zrn.at[v, 1, :, c], at_zm)
        else:
            copy(u, SZ, s, zs.at[v, rz(zf), c], zrf.at[v, :, c], at_zm)
            copy(u, SZ, s + 1, zs.at[v, rz(zp), c], zrn.at[v, 0, :, c], at_zp)

    def rsz_mid(u, h):
        v = u - 2
        s, c = RZ + 2 * h, cols(h)
        got(u, s, zrf.at[v, :, c])
        r = rz(zp if h == 0 else zm1)
        zs[v, r, c] = (s32[v, r, c] + zrf[v, :, c].astype(F32)).astype(BF16)
        if h == 0:
            copy(u, SZ, s + 1, zs.at[v, r, c], zrn.at[v, 0, :, c], at_zp)
        else:
            copy(u, SZ, s + 1, zs.at[v, r, c], zrn.at[v, 1, :, c], at_zm)

    def finish(u, h):
        v = u - 2
        c = cols(h)
        got(u, RZ + 2 * h + 1, zs.at[v, pl.ds(0, 32), c])
        total = s32[v, rz(zh), c] + zrn[v, 0, :, c].astype(F32) + zrn[v, 1, :, c].astype(F32)
        rows = pl.ds(ROWS * v, ROWS)
        out[rows, c] = base[1, rows, c] - RELAX * total

    def edge_send(it):
        state = adj if it == 0 else lam
        bsend[it, 0] = state[31:32, :]
        bsend[it, 1] = state[0:1, :]
        copy(2 * it, SEDGE, EDGE, bsend.at[it, 0], brecv.at[it, 0], {"cell": (g + 1) % 16})
        copy(2 * it, SEDGE, EDGE, bsend.at[it, 1], brecv.at[it, 1], {"cell": (g + 15) % 16})

    def edge_use(it):
        state = adj if it == 0 else lam
        got(2 * it, EDGE, brecv.at[it])
        first, last = g == 0, g == 15

        @pl.loop(0, WIDE // TILE)
        def _(n):
            c = pl.ds(pl.multiple_of(n * TILE, TILE), TILE)
            now = state[:, c]
            row = lax.broadcasted_iota(jnp.int32, now.shape, 0)
            before = jnp.where(first, 0.0, brecv[it, 0, :, c])
            after = jnp.where(last, 0.0, brecv[it, 1, :, c])
            down = jnp.where(row == 0, before, pltpu.roll(now, 1, axis=0))
            up = jnp.where(row == 31, after, pltpu.roll(now, 31, axis=0))
            pick = jnp.where(sign[:, c] > 0, up, down)
            transport = speed[c][None, :] * kappa[:, :1] * (now - pick)
            base[it, :, c] = now + RELAX * (src[:, c] - transport)

    def gathers(u, *steps):
        for step in steps:
            gather(u, step)

    incopies[0].wait()
    pack_state(0)
    pack_state(1)
    prepare()
    pl.semaphore_wait(barrier, 19)
    a2a(0)
    a2a(1)
    edge_send(0)
    incopies[1].wait()
    incopies[2].wait()
    flip(0, 1, 2, 3, 4, 5)
    own(0)
    gather(0, 0)
    edge_use(0)
    own(1)
    pack_base(0)
    pack_base(1)
    flip(6)
    gather(0, 1)
    there(0)
    there(1)
    gather(0, 2)
    flip(7)
    gather(0, 3)
    gather(1, 0)
    flip(8)
    gather(0, 4)
    gather(0, 5)
    gather(1, 1)
    gather(0, 6)
    tproduct(0, 0)
    trsx_start(0, 0)
    tproduct(0, 1)
    trsx_start(0, 1)
    gathers(1, 2, 3)
    there_use(0)
    trsx_mid(0, 0)
    trsx_mid(0, 1)
    gathers(1, 4, 5)
    there_use(1)
    gather(1, 6)
    tproduct(1, 0)
    trsx_start(1, 0)
    tproduct(1, 1)
    trsx_start(1, 1)
    trsx_fin(0)
    trsz_mid(0, 0)
    trsz_mid(0, 1)
    trsx_mid(1, 0)
    trsx_mid(1, 1)
    tfinish(0)
    gather(2, 0)
    back(0)
    trsx_fin(1)
    gather(2, 1)
    gather(2, 2)
    trsz_mid(1, 0)
    trsz_mid(1, 1)
    gather(2, 3)
    gather(2, 4)
    gather(2, 5)
    tfinish(1)
    gather(3, 0)
    gather(2, 6)
    turn(2)
    product(2, 0)
    rsx_start(2, 0)
    gather(3, 1)
    product(2, 1)
    rsx_start(2, 1)
    back(1)
    gather(3, 2)
    gather(3, 3)
    rsx_mid(2, 0)
    gather(3, 4)
    rsx_mid(2, 1)
    gather(3, 5)
    back_use(0)
    back_use(1)
    edge_send(1)
    gather(3, 6)
    turn(3)
    product(3, 0)
    rsx_start(3, 0)
    rsx_fin(2, 0)
    product(3, 1)
    rsx_start(3, 1)
    rsx_fin(2, 1)
    rsz_mid(2, 0)
    rsz_mid(2, 1)
    edge_use(1)
    rsx_mid(3, 0)
    rsx_mid(3, 1)
    finish(2, 0)
    finish(2, 1)
    rsx_fin(3, 0)
    rsx_fin(3, 1)
    rsz_mid(3, 0)
    rsz_mid(3, 1)
    finish(3, 0)
    finish(3, 1)
    for u in range(4):
        gone(u, SGATHER, xt.at[u, pl.ds(0, 15 * SUB), :])
    for u in range(2):
        gone(u, SALL, sbuf.at[u, pl.ds(0, 15)])
        gone(u, STHERE, tbuf.at[u, pl.ds(0, 15)])
        gone(u, SBACK, wbuf.at[u, pl.ds(0, 15 * ROWS)])
        gone(u, SX, pt.at[u, pl.ds(0, 3)])
        gone(u, SZ, zst.at[u, pl.ds(0, 3)])
        gone(u + 2, SX, pb.at[u, pl.ds(0, 192), :])
        gone(u + 2, SZ, zs.at[u, pl.ds(0, 48), :])
        gone(2 * u, SEDGE, bsend.at[u])


def shards(adjoint, source, collision, speed, direction, labels, conductance):
    rows, width = adjoint.shape
    table = collision.reshape(-1, width)
    vmem = pl.BlockSpec(memory_space=pltpu.VMEM)
    smem = pl.BlockSpec(memory_space=pltpu.SMEM)
    return pl.pallas_call(
        kernel,
        out_shape=jax.ShapeDtypeStruct((rows, width), F32),
        in_specs=[pl.BlockSpec(memory_space=pltpu.HBM)] * 3 + [vmem] + [smem] * 3,
        out_specs=vmem,
        scratch_shapes=[
            pltpu.VMEM((32, WIDE), F32),
            pltpu.VMEM((32, WIDE), F32),
            pltpu.VMEM((1, WIDE), jnp.int32),
            pltpu.VMEM((32, 128), F32),
            pltpu.VMEM((WIDE, WIDE), BF16),
            pltpu.VMEM((WIDE, WIDE), BF16),
            pltpu.VMEM((32, WIDE), F32),
            pltpu.VMEM((2, 32, WIDE), F32),
            pltpu.VMEM((2, 16, ROWS, 256), BF16),
            pltpu.VMEM((2, 256, 256), BF16),
            pltpu.VMEM((2, 16, ROWS, 256), BF16),
            pltpu.VMEM((2, 256, 256), BF16),
            pltpu.VMEM((2, SUB, 256), F32),
            pltpu.VMEM((2, 256, 256), BF16),
            pltpu.VMEM((2, 16, ROWS, 256), BF16),
            pltpu.VMEM((4, WIDE, 256), BF16),
            pltpu.VMEM((256, WIDE), BF16),
            pltpu.VMEM((2, 4, 4, SUB, 256), BF16),
            pltpu.VMEM((2, 2, 2, SUB, 256), BF16),
            pltpu.VMEM((2, 2, 4, SUB, 256), BF16),
            pltpu.VMEM((2, 4, SUB, 256), F32),
            pltpu.VMEM((2, 4, SUB, 256), BF16),
            pltpu.VMEM((2, SUB, 256), BF16),
            pltpu.VMEM((2, 2, SUB, 256), BF16),
            pltpu.VMEM((2, 256, WIDE), BF16),
            pltpu.VMEM((2, 2, 32, WIDE), BF16),
            pltpu.VMEM((2, 2, 64, WIDE), BF16),
            pltpu.VMEM((2, 64, WIDE), F32),
            pltpu.VMEM((2, 64, WIDE), BF16),
            pltpu.VMEM((2, ROWS, WIDE), BF16),
            pltpu.VMEM((2, 2, ROWS, WIDE), BF16),
            pltpu.VMEM((2, 2, 1, WIDE), F32),
            pltpu.VMEM((2, 2, 1, WIDE), F32),
            pltpu.SemaphoreType.DMA((4, SEND)),
            pltpu.SemaphoreType.DMA((4, RECV)),
            pltpu.SemaphoreType.DMA((3,)),
        ],
        compiler_params=pltpu.CompilerParams(collective_id=0, has_side_effects=True, vmem_limit_bytes=58 << 20),
    )(table, adjoint, source, speed, direction, labels, conductance)


def solution(mesh):
    in_specs = (
        P("cell", "mode"),
        P("cell", "mode"),
        P(None, "cell", None, "mode"),
        P("mode"),
        P("mode"),
        P("cell"),
        P(),
    )
    return jax.shard_map(shards, mesh=mesh, in_specs=in_specs, out_specs=P("cell", "mode"), check_vma=False)
```

```python
import jax
import jax.numpy as jnp
from jax import lax
from jax.experimental import pallas as pl
from jax.experimental.pallas import tpu as pltpu
from jax.sharding import PartitionSpec as P

BRANCH = 48
RELAX = 0.5
MESH = pl.DeviceIdType.MESH
F32 = jnp.float32
BF16 = jnp.bfloat16

CH = 4
R = 32 // CH
LN = 16 * R
SUB = 144
LO, HI = pl.ds(0, 80), pl.ds(80, 64)
WIDE = 2304
COLS = ((0, 1280), (1280, 1024))
TILE = 256
HERE, UP, DOWN, FAR = 0, 1, 2, 3

ALL, Z, P0, M0, P1, M1, F0, F1, CORE, RX, RZ, THERE, BACK, EDGE, RECV = 0, 1, 2, 3, 4, 5, 6, 7, 8, 9, 15, 19, 20, 21, 22
SALL, STHERE, SBACK, SGATHER, SXT, SX, SZT, SZ, SEDGE, SEND = 0, 1, 2, 3, 5, 6, 7, 8, 9, 10


def kernel(
    k_hbm, adj_hbm, src_hbm, speed_hbm, direction_hbm, labels_hbm, conductance_hbm, out,
    speed, direction, labels, conductance, adj, src, sign, kappa, kv, kt, lam, base,
    sbuf, rbuf, tbuf, trecv, base_t, wbuf, wrecv, xt, xm,
    pt, xrft, xrnt, s32t, zst, zrft, zrnt,
    pb, xrf, xrn, s32, zs, zrf, zrn, bsend, brecv,
    ssem, rsem, insem,
):
    m, g = lax.axis_index("mode"), lax.axis_index("cell")
    y, low = m // 4, m % 4
    zl, core = low // 2, low % 2
    zh, x = g // 4, g % 4
    lowz = (1 - zl) * 2 + core
    yp, ym, yf = (y + 1) % 4, (y + 3) % 4, (y + 2) % 4
    xp, xm1, xf = (x + 1) % 4, (x + 3) % 4, (x + 2) % 4
    zp, zm1, zf = (zh + 1) % 4, (zh + 3) % 4, (zh + 2) % 4
    at_yp, at_ym = {"mode": yp * 4 + low}, {"mode": ym * 4 + low}
    at_z, at_mate = {"mode": y * 4 + lowz}, {"mode": y * 4 + zl * 2 + (1 - core)}
    at_xp, at_xm = {"cell": zh * 4 + xp}, {"cell": zh * 4 + xm1}
    at_zp, at_zm = {"cell": zp * 4 + x}, {"cell": zm1 * 4 + x}
    place = x * 4 + zh
    others = [(zh + dz) % 4 * 4 + (x + dx) % 4 for dz in (2, 1, 3, 0) for dx in (2, 1, 3, 0) if dz or dx]

    def copy(u, send, recv, source, target, where):
        pltpu.make_async_remote_copy(
            src_ref=source, dst_ref=target, send_sem=ssem.at[send], recv_sem=rsem.at[u, recv],
            device_id=where, device_id_type=MESH,
        ).start()

    def got(u, recv, like):
        pltpu.make_async_copy(like, like, rsem.at[u, recv]).wait()

    def gone(send, like):
        pltpu.make_async_copy(like, like, ssem.at[send]).wait()

    barrier = pltpu.get_barrier_semaphore()
    for d in range(1, 16):
        pl.semaphore_signal(barrier, inc=1, device_id={"cell": (g + d) % 16}, device_id_type=MESH)
    for where in (at_yp, at_ym, at_z, at_mate):
        pl.semaphore_signal(barrier, inc=1, device_id=where, device_id_type=MESH)

    incopies = [
        pltpu.make_async_copy(a, b, insem.at[n])
        for n, (a, b) in enumerate((
            (adj_hbm, adj), (direction_hbm, direction), (labels_hbm, labels), (conductance_hbm, conductance),
            (speed_hbm, speed), (src_hbm, src),
        ))
    ]
    for rel, yy in ((HERE, y), (UP, yp), (DOWN, ym), (FAR, yf)):
        source = k_hbm.at[pl.ds(pl.multiple_of(yy * 4 * SUB, 16), 4 * SUB), :]
        incopies.append(pltpu.make_async_copy(source, kv.at[pl.ds(rel * 4 * SUB, 4 * SUB), :], insem.at[6 + rel]))
    for c in incopies:
        c.start()

    def await_in(*which):
        for n in which:
            incopies[n].wait()

    def prepare():
        lane = lax.broadcasted_iota(jnp.int32, (1, 128), 1)
        for t in range(WIDE // 128):
            first = t * 128 // BRANCH
            v = jnp.full((1, 128), direction[first], jnp.int32)
            for q in range(first + 1, (t * 128 + 127) // BRANCH + 1):
                v = jnp.where(lane >= q * BRANCH - t * 128, direction[q], v)
            sign[:, t * 128 : t * 128 + 128] = 2 * v - 1
        row = lax.broadcasted_iota(jnp.int32, (32, 128), 0)
        k = jnp.zeros((32, 128), F32)
        for r in range(32):
            k = jnp.where(row == r, conductance[labels[r]], k)
        kappa[...] = k


    def window(q):
        return (SUB * q) // 128 * 128, (SUB * q) % 128

    def pack(c, state, into):
        rows = pl.ds(R * c, R)
        for q in range(16):
            start, off = window(q)
            part = state[rows, start : start + 256]
            if off:
                part = pltpu.roll(part, 256 - off, axis=1)
            into[c, q] = part.astype(BF16)

    def exchange(c, send, recv, source, target):
        for to in others:
            copy(c, send, recv, source.at[c, to], target.at[c, place], {"cell": to})
        target[c, place] = source[c, g]

    def turned(v):
        return v.astype(F32).reshape(LN, 256).T[:SUB]

    def pack_state(c):
        pack(c, adj, sbuf)

    def pack_base(c):
        pack(c, base.at[0], tbuf)

    def a2a(c):
        exchange(c, SALL, ALL, sbuf, rbuf)

    def there(c):
        exchange(c, STHERE, THERE, tbuf, trecv)

    def there_use(c):
        got(c, THERE, trecv.at[c, pl.ds(0, 15)])
        base_t[c] = turned(trecv[c])

    def flip(j):
        @pl.loop(0, WIDE // TILE)
        def _(i):
            part = pl.ds(pl.multiple_of(i * TILE, TILE), TILE)
            kt[j * TILE : (j + 1) * TILE, part] = kv[part, j * TILE : (j + 1) * TILE].T

    def own(c):
        got(c, ALL, rbuf.at[c, pl.ds(0, 15)])
        xt[c, slot_rows(HERE, low), :] = turned(rbuf[c]).astype(BF16)


    def slot_rows(rel, lo):
        return pl.ds(pl.multiple_of((rel * 4 + lo) * SUB, 16), SUB)

    def blk(u, rel, lo):
        return xt.at[u, slot_rows(rel, lo), :]

    def part(u, rel, lo, p):
        start, size = (0, 80) if p == 0 else (80, 64)
        return xt.at[u, pl.ds(pl.multiple_of((rel * 4 + lo) * SUB + start, 16), size), :]

    def to_mate(u, rel, lo):
        copy(u, SGATHER + u // CH, CORE, blk(u, rel, lo), blk(u, rel, lo), at_mate)

    def gather(u, step):
        one, send = xt.at[u, pl.ds(0, SUB), :], SGATHER + u // CH
        if step in (0, 1):
            if step:
                got(u, Z, one)
            lo, p, n = (low, P0, M0) if step == 0 else (lowz, P1, M1)
            if step == 0:
                copy(u, send, Z, blk(u, HERE, low), blk(u, HERE, low), at_z)
            copy(u, send, p, blk(u, HERE, lo), blk(u, DOWN, lo), at_yp)
            copy(u, send, n, blk(u, HERE, lo), blk(u, UP, lo), at_ym)
        elif step in (2, 4):
            lo, p, far = (low, P0, F0) if step == 2 else (lowz, P1, F1)
            got(u, p, one)
            copy(u, send, far, part(u, DOWN, lo, 0), part(u, FAR, lo, 0), at_yp)
        elif step in (3, 5):
            lo, n, far = (low, M0, F0) if step == 3 else (lowz, M1, F1)
            got(u, n, one)
            copy(u, send, far, part(u, UP, lo, 1), part(u, FAR, lo, 1), at_ym)
        elif step in (6, 7):
            got(u, F0 if step == 6 else F1, one)
            to_mate(u, FAR, low if step == 6 else lowz)
        else:
            got(u, CORE, xt.at[u, pl.ds(0, 8 * SUB), :])

    def mate(u, step):
        rel = (HERE, HERE, DOWN, UP, DOWN, UP)[step]
        to_mate(u, rel, low if step in (0, 2, 3) else lowz)


    groups = (zf, zp, zm1, zh)

    def tproduct(u, p):
        for j in (2 * p, 2 * p + 1):
            rows = kt[pl.ds(pl.multiple_of(groups[j] * 4 * SUB, 64), 4 * SUB), :]
            pt[u, j] = jnp.dot(rows, xt[u], preferred_element_type=F32).astype(BF16).reshape(4, SUB, LN)
        s = RX + 3 * p
        for j in (2 * p, 2 * p + 1):
            if j % 2 == 0:
                copy(u, SXT, s, pt.at[u, j, xf], xrft.at[u, j], at_xp)
                copy(u, SXT, s + 2, pt.at[u, j, xm1], xrnt.at[u, 1, j], at_xm)
            else:
                copy(u, SXT, s + 1, pt.at[u, j, xf], xrft.at[u, j], at_xm)
                copy(u, SXT, s + 2, pt.at[u, j, xp], xrnt.at[u, 0, j], at_xp)

    def trsx_mid(u, j):
        p, d = j // 2, j % 2
        to, where = (xm1, at_xm) if d else (xp, at_xp)
        got(u, RX + 3 * p + d, xrft.at[u, j])
        pt[u, j, to] = (pt[u, j, to].astype(F32) + xrft[u, j].astype(F32)).astype(BF16)
        copy(u, SXT, RX + 3 * p + 2, pt.at[u, j, to], xrnt.at[u, d, j], where)

    def trsx_fin(u, p):
        got(u, RX + 3 * p + 2, xrnt.at[u, 0])
        for j in (2 * p, 2 * p + 1):
            total = pt[u, j, x].astype(F32) + xrnt[u, 0, j].astype(F32) + xrnt[u, 1, j].astype(F32)
            s32t[u, j] = total
            zst[u, j] = total.astype(BF16)
            if j == 0:
                copy(u, SZT, RZ, zst.at[u, 0, LO, :], zrft.at[u, LO, :], at_zp)
                copy(u, SZT, RZ + 1, zst.at[u, 0, HI, :], zrft.at[u, HI, :], at_zm)
            elif j == 1:
                copy(u, SZT, RZ + 2, zst.at[u, 1, HI, :], zrnt.at[u, 0, HI, :], at_zp)
            elif j == 2:
                copy(u, SZT, RZ + 2, zst.at[u, 2, LO, :], zrnt.at[u, 1, LO, :], at_zm)

    def trsz_mid(u, p):
        j, c, where = p + 1, HI if p else LO, at_zm if p else at_zp
        got(u, RZ + p, zrft.at[u, c, :])
        zst[u, j, c, :] = (s32t[u, j, c, :] + zrft[u, c, :].astype(F32)).astype(BF16)
        copy(u, SZT, RZ + 2, zst.at[u, j, c, :], zrnt.at[u, p, c, :], where)

    def tfinish(u):
        got(u, RZ + 2, zrnt.at[u])
        total = s32t[u, 3] + zrnt[u, 0].astype(F32) + zrnt[u, 1].astype(F32)
        new = base_t[u] - RELAX * total
        xt[u + CH, slot_rows(HERE, low), :] = new.astype(BF16)
        s32t[u, 3] = total
        gather(u + CH, 0)

    def back(u):
        total = jnp.concatenate([s32t[u, 3], jnp.zeros((256 - SUB, LN), F32)], axis=0)
        wbuf[u] = total.T.reshape(16, R, 256).astype(BF16)
        for to in others:
            copy(u, SBACK, BACK, wbuf.at[u, to % 4 * 4 + to // 4], wrecv.at[u, g], {"cell": to})
        wrecv[u, g] = wbuf[u, place]

    def back_use(u):
        got(u, BACK, wrecv.at[u, pl.ds(0, 15)])
        rows = pl.ds(R * u, R)
        lam[rows, :] = base[0, rows, :]
        for q in range(16):
            start, off = window(q)
            w = wrecv[u, q].astype(F32)
            if off:
                w = pltpu.roll(w, off, axis=1)
            lam[rows, start : start + 256] = lam[rows, start : start + 256] - RELAX * w


    def turn(u):
        @pl.loop(0, WIDE // TILE)
        def _(k):
            c = pl.ds(pl.multiple_of(k * TILE, TILE), TILE)
            xm[:, c] = xt[u, c, :].T

    def cols(h):
        return pl.ds(COLS[h][0], COLS[h][1])

    def rx(to, upper):
        return pl.ds(pl.multiple_of(to * 4 * R + upper * 2 * R, 16), 2 * R)

    def product(u, h):
        v = u - CH
        start, width = COLS[h]

        @pl.loop(0, width // TILE)
        def _(n):
            c = pl.ds(pl.multiple_of(start + n * TILE, TILE), TILE)
            pb[v, :, c] = jnp.dot(xm[...], kv[:, c], preferred_element_type=F32).astype(BF16)

        s, c, lo, hi = RX + 3 * h, cols(h), pl.ds(0, 2 * R), pl.ds(2 * R, 2 * R)
        copy(u, SX, s, pb.at[v, rx(xf, 0), c], xrf.at[v, 0, :, c], at_xp)
        copy(u, SX, s + 1, pb.at[v, rx(xf, 1), c], xrf.at[v, 1, :, c], at_xm)
        copy(u, SX, s + 2, pb.at[v, rx(xp, 1), c], xrn.at[v, 0, hi, c], at_xp)
        copy(u, SX, s + 2, pb.at[v, rx(xm1, 0), c], xrn.at[v, 1, lo, c], at_xm)

    def rsx_mid(u, h, d):
        v, s, c = u - CH, RX + 3 * h, cols(h)
        got(u, s + d, xrf.at[v, d, :, c])
        r, half, where = (rx(xm1, 1), pl.ds(2 * R, 2 * R), at_xm) if d else (rx(xp, 0), pl.ds(0, 2 * R), at_xp)
        pb[v, r, c] = (pb[v, r, c].astype(F32) + xrf[v, d, :, c].astype(F32)).astype(BF16)
        copy(u, SX, s + 2, pb.at[v, r, c], xrn.at[v, d, half, c], where)

    def rsx_fin(u, h):
        v, c, s = u - CH, cols(h), RZ + 2 * h
        got(u, RX + 3 * h + 2, pb.at[v, pl.ds(0, 8 * R), c])
        r = pl.ds(pl.multiple_of(x * 4 * R, 4 * R), 4 * R)
        total = pb[v, r, c].astype(F32) + xrn[v, 0, :, c].astype(F32) + xrn[v, 1, :, c].astype(F32)
        total = total.reshape(4, R, COLS[h][1])
        s32[v, :, :, c] = total
        zs[v, :, :, c] = total.astype(BF16)
        if h == 0:
            copy(u, SZ, s, zs.at[v, zf, :, c], zrf.at[v, :, c], at_zp)
            copy(u, SZ, s + 1, zs.at[v, zm1, :, c], zrn.at[v, 1, :, c], at_zm)
        else:
            copy(u, SZ, s, zs.at[v, zf, :, c], zrf.at[v, :, c], at_zm)
            copy(u, SZ, s + 1, zs.at[v, zp, :, c], zrn.at[v, 0, :, c], at_zp)

    def rsz_mid(u, h):
        v, c, s = u - CH, cols(h), RZ + 2 * h
        to, where = (zm1, at_zm) if h else (zp, at_zp)
        got(u, s, zrf.at[v, :, c])
        zs[v, to, :, c] = (s32[v, to, :, c] + zrf[v, :, c].astype(F32)).astype(BF16)
        copy(u, SZ, s + 1, zs.at[v, to, :, c], zrn.at[v, h, :, c], where)

    def finish(u, h):
        v, c = u - CH, cols(h)
        got(u, RZ + 2 * h + 1, zrn.at[v, :, :, c])
        total = s32[v, zh, :, c] + zrn[v, 0, :, c].astype(F32) + zrn[v, 1, :, c].astype(F32)
        rows = pl.ds(R * v, R)
        out[rows, c] = base[1, rows, c] - RELAX * total


    def edge_send(it):
        state = adj if it == 0 else lam
        bsend[it, 0] = state[31:32, :]
        bsend[it, 1] = state[0:1, :]
        copy(it, SEDGE, EDGE, bsend.at[it, 0], brecv.at[it, 0], {"cell": (g + 1) % 16})
        copy(it, SEDGE, EDGE, bsend.at[it, 1], brecv.at[it, 1], {"cell": (g + 15) % 16})

    def edge_use(it):
        state = adj if it == 0 else lam
        got(it, EDGE, brecv.at[it])
        first, last = g == 0, g == 15

        @pl.loop(0, WIDE // TILE)
        def _(n):
            c = pl.ds(pl.multiple_of(n * TILE, TILE), TILE)
            now = state[:, c]
            row = lax.broadcasted_iota(jnp.int32, now.shape, 0)
            before = jnp.where(first, 0.0, brecv[it, 0, :, c])
            after = jnp.where(last, 0.0, brecv[it, 1, :, c])
            down = jnp.where(row == 0, before, pltpu.roll(now, 1, axis=0))
            up = jnp.where(row == 31, after, pltpu.roll(now, 31, axis=0))
            pick = jnp.where(sign[:, c] > 0, up, down)
            transport = speed[c][None, :] * kappa[:, :1] * (now - pick)
            base[it, :, c] = now + RELAX * (src[:, c] - transport)

    await_in(0)
    await_in(1, 2, 3)
    pack_state(0)
    pack_state(1)
    pack_state(2)
    pack_state(3)
    prepare()
    await_in(4, 5)
    pl.semaphore_wait(barrier, 19)
    a2a(0)
    a2a(1)
    a2a(2)
    a2a(3)
    edge_send(0)
    await_in(6, 7, 8, 9)
    flip(0)
    flip(1)
    flip(2)
    flip(3)
    flip(4)
    flip(5)
    flip(6)
    own(0)
    gather(0, 0)
    mate(0, 0)
    flip(7)
    flip(8)
    edge_use(0)
    pack_base(0)
    pack_base(1)
    pack_base(2)
    pack_base(3)
    gather(0, 1)
    own(1)
    gather(1, 0)
    gather(0, 2)
    gather(0, 3)
    mate(0, 1)
    mate(0, 2)
    mate(0, 3)
    mate(1, 0)
    gather(0, 4)
    gather(0, 5)
    mate(0, 4)
    mate(0, 5)
    there(0)
    gather(1, 1)
    own(2)
    gather(2, 0)
    mate(1, 1)
    mate(2, 0)
    there(1)
    there(2)
    there(3)
    gather(1, 2)
    gather(1, 3)
    mate(1, 2)
    mate(1, 3)
    gather(0, 6)
    gather(0, 7)
    gather(2, 1)
    own(3)
    gather(3, 0)
    mate(2, 1)
    mate(3, 0)
    gather(1, 5)
    mate(1, 5)
    gather(1, 4)
    mate(1, 4)
    gather(2, 3)
    mate(2, 3)
    gather(2, 2)
    mate(2, 2)
    gather(0, 8)
    tproduct(0, 0)
    gather(1, 6)
    tproduct(0, 1)
    gather(2, 4)
    gather(2, 5)
    gather(3, 1)
    mate(2, 4)
    mate(2, 5)
    gather(3, 2)
    gather(3, 3)
    mate(3, 1)
    mate(3, 2)
    mate(3, 3)
    there_use(0)
    gather(1, 7)
    there_use(1)
    gather(2, 6)
    trsx_mid(0, 0)
    there_use(2)
    trsx_mid(0, 1)
    gather(2, 7)
    there_use(3)
    trsx_mid(0, 2)
    gather(3, 5)
    mate(3, 5)
    gather(3, 4)
    mate(3, 4)
    gather(1, 8)
    tproduct(1, 0)
    gather(2, 8)
    tproduct(2, 0)
    trsx_fin(0, 0)
    tproduct(1, 1)
    trsx_mid(0, 3)
    gather(3, 6)
    trsx_mid(1, 0)
    gather(3, 7)
    tproduct(2, 1)
    trsx_mid(1, 1)
    trsx_mid(2, 0)
    gather(3, 8)
    tproduct(3, 0)
    trsz_mid(0, 0)
    trsx_mid(2, 1)
    trsx_mid(1, 2)
    tproduct(3, 1)
    trsx_fin(0, 1)
    trsz_mid(0, 1)
    trsx_mid(1, 3)
    trsx_mid(2, 2)
    trsx_mid(2, 3)
    trsx_fin(1, 0)
    trsx_mid(3, 0)
    trsx_mid(3, 1)
    trsx_fin(2, 0)
    tfinish(0)
    mate(4, 0)
    back(0)
    trsx_mid(3, 2)
    trsx_mid(3, 3)
    trsz_mid(1, 0)
    trsx_fin(1, 1)
    trsz_mid(1, 1)
    trsx_fin(2, 1)
    gather(4, 1)
    gather(4, 2)
    gather(4, 3)
    mate(4, 1)
    mate(4, 2)
    mate(4, 3)
    trsx_fin(3, 0)
    trsz_mid(2, 1)
    trsz_mid(2, 0)
    trsx_fin(3, 1)
    gather(4, 4)
    gather(4, 5)
    mate(4, 4)
    mate(4, 5)
    tfinish(1)
    gather(4, 6)
    mate(5, 0)
    back(1)
    back_use(0)
    trsz_mid(3, 0)
    trsz_mid(3, 1)
    gather(4, 7)
    tfinish(2)
    mate(6, 0)
    back(2)
    gather(5, 1)
    gather(5, 2)
    gather(5, 3)
    mate(5, 1)
    mate(5, 2)
    mate(5, 3)
    gather(4, 8)
    turn(4)
    product(4, 0)
    gather(5, 4)
    gather(5, 5)
    gather(6, 1)
    tfinish(3)
    mate(5, 4)
    mate(5, 5)
    product(4, 1)
    gather(5, 6)
    gather(6, 2)
    gather(6, 3)
    mate(6, 1)
    mate(6, 2)
    mate(6, 3)
    mate(7, 0)
    back(3)
    back_use(1)
    back_use(2)
    gather(5, 7)
    rsx_mid(4, 0, 0)
    rsx_mid(4, 0, 1)
    gather(7, 1)
    mate(7, 1)
    gather(6, 5)
    mate(6, 5)
    gather(6, 4)
    mate(6, 4)
    gather(7, 3)
    mate(7, 3)
    gather(7, 2)
    mate(7, 2)
    rsx_mid(4, 1, 0)
    gather(6, 6)
    rsx_mid(4, 1, 1)
    gather(5, 8)
    turn(5)
    product(5, 0)
    gather(6, 7)
    product(5, 1)
    gather(7, 4)
    gather(7, 5)
    mate(7, 4)
    mate(7, 5)
    gather(7, 6)
    rsx_fin(4, 0)
    rsx_fin(4, 1)
    back_use(3)
    edge_send(1)
    gather(6, 8)
    turn(6)
    product(6, 0)
    product(6, 1)
    gather(7, 7)
    rsx_mid(5, 0, 0)
    rsx_mid(5, 0, 1)
    rsx_mid(5, 1, 0)
    rsx_mid(5, 1, 1)
    edge_use(1)
    rsz_mid(4, 0)
    rsz_mid(4, 1)
    gather(7, 8)
    turn(7)
    product(7, 0)
    product(7, 1)
    rsx_mid(6, 0, 0)
    rsx_mid(6, 0, 1)
    rsx_mid(6, 1, 0)
    rsx_mid(6, 1, 1)
    rsx_fin(5, 0)
    rsx_fin(5, 1)
    finish(4, 0)
    finish(4, 1)
    rsx_mid(7, 0, 0)
    rsx_mid(7, 0, 1)
    rsx_mid(7, 1, 0)
    rsx_mid(7, 1, 1)
    rsz_mid(5, 0)
    rsx_fin(6, 0)
    rsz_mid(5, 1)
    rsx_fin(6, 1)
    rsx_fin(7, 0)
    rsx_fin(7, 1)
    finish(5, 0)
    rsz_mid(6, 0)
    finish(5, 1)
    rsz_mid(6, 1)
    rsz_mid(7, 0)
    rsz_mid(7, 1)
    finish(6, 0)
    finish(6, 1)
    finish(7, 0)
    finish(7, 1)
    gone(SALL, sbuf.at[:, pl.ds(0, 15)])
    gone(STHERE, tbuf.at[:, pl.ds(0, 15)])
    gone(SBACK, wbuf.at[:, pl.ds(0, 15)])
    for it in range(2):
        gone(SGATHER + it, xt.at[pl.ds(it * CH, CH), pl.ds(0, 15 * SUB), :])
    gone(SXT, pt.at[:, pl.ds(0, 3)])
    gone(SX, pb.at[:, pl.ds(0, 12 * R), :])
    gone(SZT, zst.at[:, pl.ds(0, 3)])
    gone(SZ, zs.at[:, pl.ds(0, 3)])
    gone(SEDGE, bsend)


def shards(adjoint, source, collision, speed, direction, labels, conductance):
    rows, width = adjoint.shape
    table = collision.reshape(-1, width)
    return pl.pallas_call(
        kernel,
        out_shape=jax.ShapeDtypeStruct((rows, width), F32),
        in_specs=[pl.BlockSpec(memory_space=pltpu.HBM)] * 7,
        out_specs=pl.BlockSpec(memory_space=pltpu.VMEM),
        scratch_shapes=[
            pltpu.VMEM(speed.shape, F32),
            pltpu.SMEM(direction.shape, jnp.int32),
            pltpu.SMEM(labels.shape, jnp.int32),
            pltpu.SMEM(conductance.shape, F32),
            pltpu.VMEM((32, WIDE), F32),
            pltpu.VMEM((32, WIDE), F32),
            pltpu.VMEM((1, WIDE), jnp.int32),
            pltpu.VMEM((32, 128), F32),
            pltpu.VMEM((WIDE, WIDE), BF16),
            pltpu.VMEM((WIDE, WIDE), BF16),
            pltpu.VMEM((32, WIDE), F32),
            pltpu.VMEM((2, 32, WIDE), F32),
            pltpu.VMEM((CH, 16, R, 256), BF16),
            pltpu.VMEM((CH, 16, R, 256), BF16),
            pltpu.VMEM((CH, 16, R, 256), BF16),
            pltpu.VMEM((CH, 16, R, 256), BF16),
            pltpu.VMEM((CH, SUB, LN), F32),
            pltpu.VMEM((CH, 16, R, 256), BF16),
            pltpu.VMEM((CH, 16, R, 256), BF16),
            pltpu.VMEM((2 * CH, WIDE, LN), BF16),
            pltpu.VMEM((LN, WIDE), BF16),
            pltpu.VMEM((CH, 4, 4, SUB, LN), BF16),
            pltpu.VMEM((CH, 4, SUB, LN), BF16),
            pltpu.VMEM((CH, 2, 4, SUB, LN), BF16),
            pltpu.VMEM((CH, 4, SUB, LN), F32),
            pltpu.VMEM((CH, 4, SUB, LN), BF16),
            pltpu.VMEM((CH, SUB, LN), BF16),
            pltpu.VMEM((CH, 2, SUB, LN), BF16),
            pltpu.VMEM((CH, LN, WIDE), BF16),
            pltpu.VMEM((CH, 2, 2 * R, WIDE), BF16),
            pltpu.VMEM((CH, 2, 4 * R, WIDE), BF16),
            pltpu.VMEM((CH, 4, R, WIDE), F32),
            pltpu.VMEM((CH, 4, R, WIDE), BF16),
            pltpu.VMEM((CH, R, WIDE), BF16),
            pltpu.VMEM((CH, 2, R, WIDE), BF16),
            pltpu.VMEM((2, 2, 1, WIDE), F32),
            pltpu.VMEM((2, 2, 1, WIDE), F32),
            pltpu.SemaphoreType.DMA((SEND,)),
            pltpu.SemaphoreType.DMA((2 * CH, RECV)),
            pltpu.SemaphoreType.DMA((10,)),
        ],
        compiler_params=pltpu.CompilerParams(collective_id=0, has_side_effects=True, vmem_limit_bytes=58 << 20),
    )(table, adjoint, source, speed, direction, labels, conductance)


def solution(mesh):
    in_specs = (
        P("cell", "mode"),
        P("cell", "mode"),
        P(None, "cell", None, "mode"),
        P("mode"),
        P("mode"),
        P("cell"),
        P(),
    )
    return jax.shard_map(shards, mesh=mesh, in_specs=in_specs, out_specs=P("cell", "mode"), check_vma=False)
```

```python
import jax
import jax.numpy as jnp
from jax import lax
from jax.experimental import pallas as pl
from jax.experimental.pallas import tpu as pltpu
from jax.sharding import PartitionSpec as P

BRANCH = 48
RELAX = 0.5
MESH = pl.DeviceIdType.MESH
F32 = jnp.float32
BF16 = jnp.bfloat16

CH = 4
R = 32 // CH
LN = 16 * R
SUB = 144
LO, HI = pl.ds(0, 80), pl.ds(80, 64)
WIDE = 2304
COLS = ((0, 1280), (1280, 1024))
TILE = 256
HERE, UP, DOWN, FAR = 0, 1, 2, 3

ALL, Z, P0, M0, P1, M1, F0, F1, CORE, RX, RZ, THERE, BACK, EDGE, RECV = 0, 1, 2, 3, 4, 5, 6, 7, 8, 9, 15, 19, 20, 21, 22
SALL, STHERE, SBACK, SGATHER, SXT, SX, SZT, SZ, SEDGE, SEND = 0, 1, 2, 3, 5, 6, 7, 8, 9, 10


def kernel(
    k_hbm, adj_hbm, src_hbm, speed_hbm, direction_hbm, labels_hbm, conductance_hbm, out,
    speed, direction, labels, conductance, adj, src, sign, kappa, kv, kt, lam, base,
    sbuf, rbuf, tbuf, trecv, base_t, wbuf, wrecv, xt, xm,
    pt, xrft, xrnt, s32t, zst, zrft, zrnt,
    pb, xrf, xrn, s32, zs, zrf, zrn, bsend, brecv,
    ssem, rsem, insem,
):
    m, g = lax.axis_index("mode"), lax.axis_index("cell")
    y, low = m // 4, m % 4
    zl, core = low // 2, low % 2
    zh, x = g // 4, g % 4
    lowz = (1 - zl) * 2 + core
    yp, ym, yf = (y + 1) % 4, (y + 3) % 4, (y + 2) % 4
    xp, xm1, xf = (x + 1) % 4, (x + 3) % 4, (x + 2) % 4
    zp, zm1, zf = (zh + 1) % 4, (zh + 3) % 4, (zh + 2) % 4
    at_yp, at_ym = {"mode": yp * 4 + low}, {"mode": ym * 4 + low}
    lowm = zl * 2 + (1 - core)
    at_z, at_mate = {"mode": y * 4 + lowz}, {"mode": y * 4 + lowm}
    at_yp2, at_ym2 = {"mode": yp * 4 + lowm}, {"mode": ym * 4 + lowm}
    at_xp, at_xm = {"cell": zh * 4 + xp}, {"cell": zh * 4 + xm1}
    at_zp, at_zm = {"cell": zp * 4 + x}, {"cell": zm1 * 4 + x}
    place = x * 4 + zh
    others = [(zh + dz) % 4 * 4 + (x + dx) % 4 for dz in (2, 1, 3, 0) for dx in (2, 1, 3, 0) if dz or dx]

    def copy(u, send, recv, source, target, where):
        pltpu.make_async_remote_copy(
            src_ref=source, dst_ref=target, send_sem=ssem.at[send], recv_sem=rsem.at[u, recv],
            device_id=where, device_id_type=MESH,
        ).start()

    def got(u, recv, like):
        pltpu.make_async_copy(like, like, rsem.at[u, recv]).wait()

    def gone(send, like):
        pltpu.make_async_copy(like, like, ssem.at[send]).wait()

    barrier = pltpu.get_barrier_semaphore()
    for d in range(1, 16):
        pl.semaphore_signal(barrier, inc=1, device_id={"cell": (g + d) % 16}, device_id_type=MESH)
    for where in (at_yp, at_ym, at_z, at_mate, at_yp2, at_ym2):
        pl.semaphore_signal(barrier, inc=1, device_id=where, device_id_type=MESH)

    incopies = [
        pltpu.make_async_copy(a, b, insem.at[n])
        for n, (a, b) in enumerate((
            (adj_hbm, adj), (direction_hbm, direction), (labels_hbm, labels), (conductance_hbm, conductance),
            (speed_hbm, speed), (src_hbm, src),
        ))
    ]
    for rel, yy in ((HERE, y), (UP, yp), (DOWN, ym), (FAR, yf)):
        source = k_hbm.at[pl.ds(pl.multiple_of(yy * 4 * SUB, 16), 4 * SUB), :]
        incopies.append(pltpu.make_async_copy(source, kv.at[pl.ds(rel * 4 * SUB, 4 * SUB), :], insem.at[6 + rel]))
    for c in incopies:
        c.start()

    def await_in(*which):
        for n in which:
            incopies[n].wait()

    def prepare():
        lane = lax.broadcasted_iota(jnp.int32, (1, 128), 1)
        for t in range(WIDE // 128):
            first = t * 128 // BRANCH
            v = jnp.full((1, 128), direction[first], jnp.int32)
            for q in range(first + 1, (t * 128 + 127) // BRANCH + 1):
                v = jnp.where(lane >= q * BRANCH - t * 128, direction[q], v)
            sign[:, t * 128 : t * 128 + 128] = 2 * v - 1
        row = lax.broadcasted_iota(jnp.int32, (32, 128), 0)
        k = jnp.zeros((32, 128), F32)
        for r in range(32):
            k = jnp.where(row == r, conductance[labels[r]], k)
        kappa[...] = k


    def window(q):
        return (SUB * q) // 128 * 128, (SUB * q) % 128

    def pack(c, state, into):
        rows = pl.ds(R * c, R)
        for q in range(16):
            start, off = window(q)
            part = state[rows, start : start + 256]
            if off:
                part = pltpu.roll(part, 256 - off, axis=1)
            into[c, q] = part.astype(BF16)

    def exchange(c, send, recv, source, target):
        for to in others:
            copy(c, send, recv, source.at[c, to], target.at[c, place], {"cell": to})
        target[c, place] = source[c, g]

    def turned(v):
        return v.astype(F32).reshape(LN, 256).T[:SUB]

    def pack_state(c):
        pack(c, adj, sbuf)

    def pack_base(c):
        pack(c, base.at[0], tbuf)

    def a2a(c):
        exchange(c, SALL, ALL, sbuf, rbuf)

    def there(c):
        exchange(c, STHERE, THERE, tbuf, trecv)

    def there_use(c):
        got(c, THERE, trecv.at[c, pl.ds(0, 15)])
        base_t[c] = turned(trecv[c])

    def flip(j):
        @pl.loop(0, WIDE // TILE)
        def _(i):
            part = pl.ds(pl.multiple_of(i * TILE, TILE), TILE)
            kt[j * TILE : (j + 1) * TILE, part] = kv[part, j * TILE : (j + 1) * TILE].T

    def own(c):
        got(c, ALL, rbuf.at[c, pl.ds(0, 15)])
        xt[c, slot_rows(HERE, low), :] = turned(rbuf[c]).astype(BF16)


    def slot_rows(rel, lo):
        return pl.ds(pl.multiple_of((rel * 4 + lo) * SUB, 16), SUB)

    def blk(u, rel, lo):
        return xt.at[u, slot_rows(rel, lo), :]

    def part(u, rel, lo, p):
        start, size = (0, 80) if p == 0 else (80, 64)
        return xt.at[u, pl.ds(pl.multiple_of((rel * 4 + lo) * SUB + start, 16), size), :]

    def gather(u, step):
        one, send = xt.at[u, pl.ds(0, SUB), :], SGATHER + u // CH
        if step in (0, 1):
            if step:
                got(u, Z, one)
            lo, p, n = (low, P0, M0) if step == 0 else (lowz, P1, M1)
            if step == 0:
                copy(u, send, Z, blk(u, HERE, low), blk(u, HERE, low), at_z)
            copy(u, send, p, blk(u, HERE, lo), blk(u, DOWN, lo), at_yp)
            copy(u, send, n, blk(u, HERE, lo), blk(u, UP, lo), at_ym)
        elif step in (2, 4):
            lo, p, far = (low, P0, F0) if step == 2 else (lowz, P1, F1)
            got(u, p, one)
            copy(u, send, far, part(u, DOWN, lo, 0), part(u, FAR, lo, 0), at_yp)
            copy(u, send, CORE, part(u, DOWN, lo, 0), part(u, FAR, lo, 0), at_yp2)
        elif step in (3, 5):
            lo, n, far = (low, M0, F0) if step == 3 else (lowz, M1, F1)
            got(u, n, one)
            copy(u, send, far, part(u, UP, lo, 1), part(u, FAR, lo, 1), at_ym)
            copy(u, send, CORE, part(u, UP, lo, 1), part(u, FAR, lo, 1), at_ym2)
        else:
            got(u, F0, one)
            got(u, F1, one)
            got(u, CORE, xt.at[u, pl.ds(0, 8 * SUB), :])

    def cross(u, step):
        lo, send = (low, lowz)[step], SGATHER + u // CH
        copy(u, send, CORE, blk(u, HERE, lo), blk(u, DOWN, lo), at_yp2)
        copy(u, send, CORE, blk(u, HERE, lo), blk(u, UP, lo), at_ym2)
        copy(u, send, CORE, blk(u, HERE, lo), blk(u, HERE, lo), at_mate)


    groups = (zf, zp, zm1, zh)

    def tproduct(u, j):
        for half in range(2):
            rows = kt[pl.ds(pl.multiple_of((groups[j] * 4 + half * 2) * SUB, 32), 2 * SUB), :]
            part = jnp.dot(rows, xt[u], preferred_element_type=F32)
            pt[u, j, pl.ds(2 * half, 2)] = part.astype(BF16).reshape(2, SUB, LN)
        s = RX + 3 * (j // 2)
        if j % 2 == 0:
            copy(u, SXT, s, pt.at[u, j, xf], xrft.at[u, j], at_xp)
            copy(u, SXT, s + 2, pt.at[u, j, xm1], xrnt.at[u, 1, j], at_xm)
        else:
            copy(u, SXT, s + 1, pt.at[u, j, xf], xrft.at[u, j], at_xm)
            copy(u, SXT, s + 2, pt.at[u, j, xp], xrnt.at[u, 0, j], at_xp)

    def trsx_mid(u, j):
        p, d = j // 2, j % 2
        to, where = (xm1, at_xm) if d else (xp, at_xp)
        got(u, RX + 3 * p + d, xrft.at[u, j])
        pt[u, j, to] = (pt[u, j, to].astype(F32) + xrft[u, j].astype(F32)).astype(BF16)
        copy(u, SXT, RX + 3 * p + 2, pt.at[u, j, to], xrnt.at[u, d, j], where)

    def trsx_fin(u, p):
        got(u, RX + 3 * p + 2, xrnt.at[u, 0])
        for j in (2 * p, 2 * p + 1):
            total = pt[u, j, x].astype(F32) + xrnt[u, 0, j].astype(F32) + xrnt[u, 1, j].astype(F32)
            s32t[u, j] = total
            zst[u, j] = total.astype(BF16)
            if j == 0:
                copy(u, SZT, RZ, zst.at[u, 0, LO, :], zrft.at[u, LO, :], at_zp)
                copy(u, SZT, RZ + 1, zst.at[u, 0, HI, :], zrft.at[u, HI, :], at_zm)
            elif j == 1:
                copy(u, SZT, RZ + 2, zst.at[u, 1, HI, :], zrnt.at[u, 0, HI, :], at_zp)
            elif j == 2:
                copy(u, SZT, RZ + 2, zst.at[u, 2, LO, :], zrnt.at[u, 1, LO, :], at_zm)

    def trsz_mid(u, p):
        j, c, where = p + 1, HI if p else LO, at_zm if p else at_zp
        got(u, RZ + p, zrft.at[u, c, :])
        zst[u, j, c, :] = (s32t[u, j, c, :] + zrft[u, c, :].astype(F32)).astype(BF16)
        copy(u, SZT, RZ + 2, zst.at[u, j, c, :], zrnt.at[u, p, c, :], where)

    def tfinish(u):
        got(u, RZ + 2, zrnt.at[u])
        total = s32t[u, 3] + zrnt[u, 0].astype(F32) + zrnt[u, 1].astype(F32)
        new = base_t[u] - RELAX * total
        xt[u + CH, slot_rows(HERE, low), :] = new.astype(BF16)
        s32t[u, 3] = total
        gather(u + CH, 0)

    def back(u):
        total = jnp.concatenate([s32t[u, 3], jnp.zeros((256 - SUB, LN), F32)], axis=0)
        wbuf[u] = total.T.reshape(16, R, 256).astype(BF16)
        for to in others:
            copy(u, SBACK, BACK, wbuf.at[u, to % 4 * 4 + to // 4], wrecv.at[u, g], {"cell": to})
        wrecv[u, g] = wbuf[u, place]

    def back_use(u):
        got(u, BACK, wrecv.at[u, pl.ds(0, 15)])
        rows = pl.ds(R * u, R)
        lam[rows, :] = base[0, rows, :]
        for q in range(16):
            start, off = window(q)
            w = wrecv[u, q].astype(F32)
            if off:
                w = pltpu.roll(w, off, axis=1)
            lam[rows, start : start + 256] = lam[rows, start : start + 256] - RELAX * w


    def turn(u):
        @pl.loop(0, WIDE // TILE)
        def _(k):
            c = pl.ds(pl.multiple_of(k * TILE, TILE), TILE)
            xm[:, c] = xt[u, c, :].T

    def cols(h):
        return pl.ds(COLS[h][0], COLS[h][1])

    def rx(to, upper):
        return pl.ds(pl.multiple_of(to * 4 * R + upper * 2 * R, 16), 2 * R)

    def product(u, h):
        v = u - CH
        start, width = COLS[h]

        wide = start + width // TILE // 2 * 2 * TILE

        @pl.loop(start // TILE, wide // TILE, step=2)
        def _(n):
            c = pl.ds(pl.multiple_of(n * TILE, TILE), 2 * TILE)
            pb[v, :, c] = jnp.dot(xm[...], kv[:, c], preferred_element_type=F32).astype(BF16)

        if wide < start + width:
            for c in (pl.ds(wide, 128), pl.ds(wide + 128, 128)):
                pb[v, :, c] = jnp.dot(xm[...], kv[:, c], preferred_element_type=F32).astype(BF16)

        s, c, lo, hi = RX + 3 * h, cols(h), pl.ds(0, 2 * R), pl.ds(2 * R, 2 * R)
        copy(u, SX, s, pb.at[v, rx(xf, 0), c], xrf.at[v, 0, :, c], at_xp)
        copy(u, SX, s + 1, pb.at[v, rx(xf, 1), c], xrf.at[v, 1, :, c], at_xm)
        copy(u, SX, s + 2, pb.at[v, rx(xp, 1), c], xrn.at[v, 0, hi, c], at_xp)
        copy(u, SX, s + 2, pb.at[v, rx(xm1, 0), c], xrn.at[v, 1, lo, c], at_xm)

    def rsx_mid(u, h, d):
        v, s, c = u - CH, RX + 3 * h, cols(h)
        got(u, s + d, xrf.at[v, d, :, c])
        r, half, where = (rx(xm1, 1), pl.ds(2 * R, 2 * R), at_xm) if d else (rx(xp, 0), pl.ds(0, 2 * R), at_xp)
        pb[v, r, c] = (pb[v, r, c].astype(F32) + xrf[v, d, :, c].astype(F32)).astype(BF16)
        copy(u, SX, s + 2, pb.at[v, r, c], xrn.at[v, d, half, c], where)

    def rsx_fin(u, h):
        v, c, s = u - CH, cols(h), RZ + 2 * h
        got(u, RX + 3 * h + 2, pb.at[v, pl.ds(0, 8 * R), c])
        r = pl.ds(pl.multiple_of(x * 4 * R, 4 * R), 4 * R)
        total = pb[v, r, c].astype(F32) + xrn[v, 0, :, c].astype(F32) + xrn[v, 1, :, c].astype(F32)
        total = total.reshape(4, R, COLS[h][1])
        s32[v, :, :, c] = total
        zs[v, :, :, c] = total.astype(BF16)
        if h == 0:
            copy(u, SZ, s, zs.at[v, zf, :, c], zrf.at[v, :, c], at_zp)
            copy(u, SZ, s + 1, zs.at[v, zm1, :, c], zrn.at[v, 1, :, c], at_zm)
        else:
            copy(u, SZ, s, zs.at[v, zf, :, c], zrf.at[v, :, c], at_zm)
            copy(u, SZ, s + 1, zs.at[v, zp, :, c], zrn.at[v, 0, :, c], at_zp)

    def rsz_mid(u, h):
        v, c, s = u - CH, cols(h), RZ + 2 * h
        to, where = (zm1, at_zm) if h else (zp, at_zp)
        got(u, s, zrf.at[v, :, c])
        zs[v, to, :, c] = (s32[v, to, :, c] + zrf[v, :, c].astype(F32)).astype(BF16)
        copy(u, SZ, s + 1, zs.at[v, to, :, c], zrn.at[v, h, :, c], where)

    def finish(u, h):
        v, c = u - CH, cols(h)
        got(u, RZ + 2 * h + 1, zrn.at[v, :, :, c])
        total = s32[v, zh, :, c] + zrn[v, 0, :, c].astype(F32) + zrn[v, 1, :, c].astype(F32)
        rows = pl.ds(R * v, R)
        out[rows, c] = base[1, rows, c] - RELAX * total


    def edge_send(it):
        state = adj if it == 0 else lam
        bsend[it, 0] = state[31:32, :]
        bsend[it, 1] = state[0:1, :]
        copy(it, SEDGE, EDGE, bsend.at[it, 0], brecv.at[it, 0], {"cell": (g + 1) % 16})
        copy(it, SEDGE, EDGE, bsend.at[it, 1], brecv.at[it, 1], {"cell": (g + 15) % 16})

    def edge_use(it):
        state = adj if it == 0 else lam
        got(it, EDGE, brecv.at[it])
        first, last = g == 0, g == 15

        @pl.loop(0, WIDE // TILE)
        def _(n):
            c = pl.ds(pl.multiple_of(n * TILE, TILE), TILE)
            now = state[:, c]
            row = lax.broadcasted_iota(jnp.int32, now.shape, 0)
            before = jnp.where(first, 0.0, brecv[it, 0, :, c])
            after = jnp.where(last, 0.0, brecv[it, 1, :, c])
            down = jnp.where(row == 0, before, pltpu.roll(now, 1, axis=0))
            up = jnp.where(row == 31, after, pltpu.roll(now, 31, axis=0))
            pick = jnp.where(sign[:, c] > 0, up, down)
            transport = speed[c][None, :] * kappa[:, :1] * (now - pick)
            base[it, :, c] = now + RELAX * (src[:, c] - transport)

    await_in(0)
    pack_state(0)
    pack_state(2)
    pack_state(1)
    pack_state(3)
    await_in(1, 2, 3)
    prepare()
    await_in(4, 5)
    pl.semaphore_wait(barrier, 21)
    a2a(0)
    edge_send(0)
    a2a(1)
    a2a(2)
    a2a(3)
    await_in(6, 7, 8, 9)
    flip(4)
    flip(3)
    flip(1)
    flip(0)
    flip(6)
    flip(5)
    edge_use(0)
    own(0)
    gather(0, 0)
    cross(0, 0)
    pack_base(0)
    pack_base(2)
    flip(2)
    flip(7)
    pack_base(1)
    flip(8)
    pack_base(3)
    gather(0, 3)
    gather(0, 1)
    own(1)
    gather(0, 2)
    cross(0, 1)
    gather(1, 0)
    cross(1, 0)
    gather(0, 4)
    gather(1, 1)
    cross(1, 1)
    gather(0, 5)
    gather(1, 3)
    own(2)
    gather(2, 0)
    cross(2, 0)
    gather(1, 2)
    gather(1, 5)
    there(1)
    there(2)
    there(0)
    there(3)
    gather(1, 4)
    gather(0, 8)
    tproduct(0, 0)
    gather(2, 1)
    cross(2, 1)
    tproduct(0, 1)
    gather(2, 3)
    gather(2, 2)
    own(3)
    tproduct(0, 2)
    gather(3, 0)
    cross(3, 0)
    tproduct(0, 3)
    gather(1, 8)
    tproduct(1, 0)
    tproduct(1, 1)
    trsx_mid(0, 0)
    gather(2, 4)
    gather(2, 5)
    trsx_mid(0, 1)
    tproduct(1, 2)
    trsx_mid(0, 2)
    there_use(2)
    tproduct(1, 3)
    trsx_mid(0, 3)
    gather(3, 3)
    gather(3, 2)
    there_use(1)
    gather(3, 1)
    cross(3, 1)
    there_use(0)
    trsx_mid(1, 0)
    trsx_mid(1, 1)
    gather(2, 8)
    tproduct(2, 0)
    tproduct(2, 1)
    trsx_mid(1, 2)
    trsx_fin(0, 0)
    tproduct(2, 2)
    tproduct(2, 3)
    trsx_fin(0, 1)
    gather(3, 4)
    trsx_mid(1, 3)
    there_use(3)
    gather(3, 5)
    trsx_fin(1, 0)
    trsx_mid(2, 0)
    trsx_mid(2, 1)
    trsz_mid(0, 1)
    trsz_mid(0, 0)
    gather(3, 8)
    tproduct(3, 0)
    trsx_mid(2, 3)
    trsx_mid(2, 2)
    tproduct(3, 1)
    trsx_fin(2, 0)
    trsx_fin(1, 1)
    trsz_mid(1, 1)
    trsz_mid(1, 0)
    tproduct(3, 2)
    tproduct(3, 3)
    tfinish(0)
    cross(4, 0)
    back(0)
    trsx_mid(3, 0)
    trsx_fin(2, 1)
    trsx_mid(3, 1)
    trsz_mid(2, 1)
    trsz_mid(2, 0)
    trsx_mid(3, 2)
    gather(4, 2)
    gather(4, 3)
    trsx_mid(3, 3)
    gather(4, 1)
    cross(4, 1)
    tfinish(1)
    back(1)
    cross(5, 0)
    trsx_fin(3, 0)
    trsx_fin(3, 1)
    gather(5, 1)
    cross(5, 1)
    gather(4, 5)
    gather(4, 4)
    tfinish(2)
    back_use(0)
    back(2)
    cross(6, 0)
    gather(5, 3)
    gather(5, 2)
    trsz_mid(3, 0)
    gather(5, 5)
    trsz_mid(3, 1)
    gather(5, 4)
    gather(6, 1)
    cross(6, 1)
    back_use(1)
    gather(4, 8)
    turn(4)
    product(4, 0)
    product(4, 1)
    gather(6, 2)
    gather(6, 3)
    tfinish(3)
    cross(7, 0)
    back_use(2)
    gather(5, 8)
    turn(5)
    gather(6, 5)
    product(5, 0)
    product(5, 1)
    gather(7, 1)
    gather(6, 4)
    cross(7, 1)
    rsx_mid(4, 0, 1)
    rsx_mid(4, 0, 0)
    back(3)
    rsx_mid(4, 1, 0)
    rsx_mid(4, 1, 1)
    gather(7, 3)
    gather(7, 2)
    rsx_mid(5, 0, 1)
    rsx_mid(5, 0, 0)
    gather(7, 5)
    gather(7, 4)
    rsx_mid(5, 1, 0)
    rsx_mid(5, 1, 1)
    gather(6, 8)
    turn(6)
    product(6, 0)
    rsx_fin(4, 0)
    product(6, 1)
    rsx_fin(4, 1)
    gather(7, 8)
    turn(7)
    product(7, 0)
    product(7, 1)
    back_use(3)
    edge_send(1)
    rsx_fin(5, 1)
    rsx_mid(6, 0, 0)
    rsx_fin(5, 0)
    rsx_mid(6, 0, 1)
    rsz_mid(4, 0)
    rsx_mid(6, 1, 1)
    rsx_mid(6, 1, 0)
    rsz_mid(4, 1)
    rsx_mid(7, 0, 1)
    rsx_mid(7, 0, 0)
    rsx_mid(7, 1, 0)
    rsx_mid(7, 1, 1)
    rsz_mid(5, 1)
    edge_use(1)
    rsz_mid(5, 0)
    rsx_fin(6, 0)
    finish(4, 1)
    finish(4, 0)
    rsx_fin(6, 1)
    rsx_fin(7, 0)
    rsx_fin(7, 1)
    finish(5, 1)
    finish(5, 0)
    rsz_mid(6, 0)
    rsz_mid(6, 1)
    rsz_mid(7, 0)
    rsz_mid(7, 1)
    finish(6, 1)
    finish(6, 0)
    finish(7, 1)
    finish(7, 0)
    gone(SALL, sbuf.at[:, pl.ds(0, 15)])
    gone(STHERE, tbuf.at[:, pl.ds(0, 15)])
    gone(SBACK, wbuf.at[:, pl.ds(0, 15)])
    for it in range(2):
        gone(SGATHER + it, xt.at[pl.ds(it * CH, CH), pl.ds(0, 15 * SUB), :])
    gone(SXT, pt.at[:, pl.ds(0, 3)])
    gone(SX, pb.at[:, pl.ds(0, 12 * R), :])
    gone(SZT, zst.at[:, pl.ds(0, 3)])
    gone(SZ, zs.at[:, pl.ds(0, 3)])
    gone(SEDGE, bsend)


def shards(adjoint, source, collision, speed, direction, labels, conductance):
    rows, width = adjoint.shape
    table = collision.reshape(-1, width)
    return pl.pallas_call(
        kernel,
        out_shape=jax.ShapeDtypeStruct((rows, width), F32),
        in_specs=[pl.BlockSpec(memory_space=pltpu.HBM)] * 7,
        out_specs=pl.BlockSpec(memory_space=pltpu.VMEM),
        scratch_shapes=[
            pltpu.VMEM(speed.shape, F32),
            pltpu.SMEM(direction.shape, jnp.int32),
            pltpu.SMEM(labels.shape, jnp.int32),
            pltpu.SMEM(conductance.shape, F32),
            pltpu.VMEM((32, WIDE), F32),
            pltpu.VMEM((32, WIDE), F32),
            pltpu.VMEM((1, WIDE), jnp.int32),
            pltpu.VMEM((32, 128), F32),
            pltpu.VMEM((WIDE, WIDE), BF16),
            pltpu.VMEM((WIDE, WIDE), BF16),
            pltpu.VMEM((32, WIDE), F32),
            pltpu.VMEM((2, 32, WIDE), F32),
            pltpu.VMEM((CH, 16, R, 256), BF16),
            pltpu.VMEM((CH, 16, R, 256), BF16),
            pltpu.VMEM((CH, 16, R, 256), BF16),
            pltpu.VMEM((CH, 16, R, 256), BF16),
            pltpu.VMEM((CH, SUB, LN), F32),
            pltpu.VMEM((CH, 16, R, 256), BF16),
            pltpu.VMEM((CH, 16, R, 256), BF16),
            pltpu.VMEM((2 * CH, WIDE, LN), BF16),
            pltpu.VMEM((LN, WIDE), BF16),
            pltpu.VMEM((CH, 4, 4, SUB, LN), BF16),
            pltpu.VMEM((CH, 4, SUB, LN), BF16),
            pltpu.VMEM((CH, 2, 4, SUB, LN), BF16),
            pltpu.VMEM((CH, 4, SUB, LN), F32),
            pltpu.VMEM((CH, 4, SUB, LN), BF16),
            pltpu.VMEM((CH, SUB, LN), BF16),
            pltpu.VMEM((CH, 2, SUB, LN), BF16),
            pltpu.VMEM((CH, LN, WIDE), BF16),
            pltpu.VMEM((CH, 2, 2 * R, WIDE), BF16),
            pltpu.VMEM((CH, 2, 4 * R, WIDE), BF16),
            pltpu.VMEM((CH, 4, R, WIDE), F32),
            pltpu.VMEM((CH, 4, R, WIDE), BF16),
            pltpu.VMEM((CH, R, WIDE), BF16),
            pltpu.VMEM((CH, 2, R, WIDE), BF16),
            pltpu.VMEM((2, 2, 1, WIDE), F32),
            pltpu.VMEM((2, 2, 1, WIDE), F32),
            pltpu.SemaphoreType.DMA((SEND,)),
            pltpu.SemaphoreType.DMA((2 * CH, RECV)),
            pltpu.SemaphoreType.DMA((10,)),
        ],
        compiler_params=pltpu.CompilerParams(collective_id=0, has_side_effects=True, vmem_limit_bytes=58 << 20),
    )(table, adjoint, source, speed, direction, labels, conductance)


def solution(mesh):
    in_specs = (
        P("cell", "mode"),
        P("cell", "mode"),
        P(None, "cell", None, "mode"),
        P("mode"),
        P("mode"),
        P("cell"),
        P(),
    )
    return jax.shard_map(shards, mesh=mesh, in_specs=in_specs, out_specs=P("cell", "mode"), check_vma=False)
```

```python
import jax
import jax.numpy as jnp
from jax import lax
from jax.experimental import pallas as pl
from jax.experimental.pallas import tpu as pltpu
from jax.sharding import PartitionSpec as P

BRANCH = 48
RELAX = 0.5
MESH = pl.DeviceIdType.MESH
F32 = jnp.float32
BF16 = jnp.bfloat16

CH = 4
R = 32 // CH
LN = 16 * R
SUB = 144
LO, HI = pl.ds(0, 80), pl.ds(80, 64)
WIDE = 2304
COLS = ((0, 1280), (1280, 1024))
TILE = 256
HERE, UP, DOWN, FAR = 0, 1, 2, 3

ALL, Z, P0, M0, P1, M1, F0, F1, CORE, RX, RZ, THERE, BACK, EDGE, RECV = 0, 1, 2, 3, 4, 5, 6, 7, 8, 9, 15, 19, 20, 21, 22
SALL, STHERE, SBACK, SGATHER, SXT, SX, SZT, SZ, SEDGE, SEND = 0, 1, 2, 3, 5, 6, 7, 8, 9, 10


def kernel(
    k_hbm, adj_hbm, src_hbm, speed_hbm, direction_hbm, labels_hbm, conductance_hbm, out,
    speed, direction, labels, conductance, adj, src, sign, kappa, kv, kt, lam, base,
    sbuf, rbuf, tbuf, trecv, base_t, wbuf, wrecv, xt, xm,
    pt, xrft, xrnt, s32t, zst, zrft, zrnt,
    pb, xrf, xrn, s32, zs, zrf, zrn, bsend, brecv,
    ssem, rsem, insem,
):
    m, g = lax.axis_index("mode"), lax.axis_index("cell")
    y, low = m // 4, m % 4
    zl, core = low // 2, low % 2
    zh, x = g // 4, g % 4
    lowz = (1 - zl) * 2 + core
    yp, ym, yf = (y + 1) % 4, (y + 3) % 4, (y + 2) % 4
    xp, xm1, xf = (x + 1) % 4, (x + 3) % 4, (x + 2) % 4
    zp, zm1, zf = (zh + 1) % 4, (zh + 3) % 4, (zh + 2) % 4
    at_yp, at_ym = {"mode": yp * 4 + low}, {"mode": ym * 4 + low}
    lowm = zl * 2 + (1 - core)
    at_z, at_mate = {"mode": y * 4 + lowz}, {"mode": y * 4 + lowm}
    at_yp2, at_ym2 = {"mode": yp * 4 + lowm}, {"mode": ym * 4 + lowm}
    at_xp, at_xm = {"cell": zh * 4 + xp}, {"cell": zh * 4 + xm1}
    at_zp, at_zm = {"cell": zp * 4 + x}, {"cell": zm1 * 4 + x}
    place = x * 4 + zh
    others = [(zh + dz) % 4 * 4 + (x + dx) % 4 for dz in (2, 1, 3, 0) for dx in (2, 1, 3, 0) if dz or dx]

    def copy(u, send, recv, source, target, where):
        pltpu.make_async_remote_copy(
            src_ref=source, dst_ref=target, send_sem=ssem.at[send], recv_sem=rsem.at[u, recv],
            device_id=where, device_id_type=MESH,
        ).start()

    def got(u, recv, like):
        pltpu.make_async_copy(like, like, rsem.at[u, recv]).wait()

    def gone(send, like):
        pltpu.make_async_copy(like, like, ssem.at[send]).wait()

    barrier = pltpu.get_barrier_semaphore()
    for d in range(1, 16):
        pl.semaphore_signal(barrier, inc=1, device_id={"cell": (g + d) % 16}, device_id_type=MESH)
    for where in (at_yp, at_ym, at_z, at_mate, at_yp2, at_ym2):
        pl.semaphore_signal(barrier, inc=1, device_id=where, device_id_type=MESH)

    incopies = [
        pltpu.make_async_copy(a, b, insem.at[n])
        for n, (a, b) in enumerate((
            (adj_hbm, adj), (direction_hbm, direction), (labels_hbm, labels), (conductance_hbm, conductance),
            (speed_hbm, speed), (src_hbm, src),
        ))
    ]
    for rel, yy in ((HERE, y), (UP, yp), (DOWN, ym), (FAR, yf)):
        source = k_hbm.at[pl.ds(pl.multiple_of(yy * 4 * SUB, 16), 4 * SUB), :]
        incopies.append(pltpu.make_async_copy(source, kv.at[pl.ds(rel * 4 * SUB, 4 * SUB), :], insem.at[6 + rel]))
    for c in incopies:
        c.start()

    def await_in(*which):
        for n in which:
            incopies[n].wait()

    def prepare():
        lane = lax.broadcasted_iota(jnp.int32, (1, 128), 1)
        for t in range(WIDE // 128):
            first = t * 128 // BRANCH
            v = jnp.full((1, 128), direction[first], jnp.int32)
            for q in range(first + 1, (t * 128 + 127) // BRANCH + 1):
                v = jnp.where(lane >= q * BRANCH - t * 128, direction[q], v)
            sign[:, t * 128 : t * 128 + 128] = 2 * v - 1
        row = lax.broadcasted_iota(jnp.int32, (32, 128), 0)
        k = jnp.zeros((32, 128), F32)
        for r in range(32):
            k = jnp.where(row == r, conductance[labels[r]], k)
        kappa[...] = k


    def window(q):
        return (SUB * q) // 128 * 128, (SUB * q) % 128

    def pack(c, state, into):
        rows = pl.ds(R * c, R)
        for q in range(16):
            start, off = window(q)
            part = state[rows, start : start + 256]
            if off:
                part = pltpu.roll(part, 256 - off, axis=1)
            into[c, q] = part.astype(BF16)

    def exchange(c, send, recv, source, target):
        for to in others:
            copy(c, send, recv, source.at[c, to], target.at[c, place], {"cell": to})
        target[c, place] = source[c, g]

    def turned(v):
        return v.astype(F32).reshape(LN, 256).T[:SUB]

    def pack_state(c):
        pack(c, adj, sbuf)

    def pack_base(c):
        pack(c, base.at[0], tbuf)

    def a2a(c):
        exchange(c, SALL, ALL, sbuf, rbuf)

    def there(c):
        exchange(c, STHERE, THERE, tbuf, trecv)

    def there_use(c):
        got(c, THERE, trecv.at[c, pl.ds(0, 15)])
        base_t[c] = turned(trecv[c])

    def flip(j):
        @pl.loop(0, WIDE // TILE)
        def _(i):
            part = pl.ds(pl.multiple_of(i * TILE, TILE), TILE)
            kt[j * TILE : (j + 1) * TILE, part] = kv[part, j * TILE : (j + 1) * TILE].T

    def own(c):
        got(c, ALL, rbuf.at[c, pl.ds(0, 15)])
        xt[c, slot_rows(HERE, low), :] = turned(rbuf[c]).astype(BF16)


    def slot_rows(rel, lo):
        return pl.ds(pl.multiple_of((rel * 4 + lo) * SUB, 16), SUB)

    def blk(u, rel, lo):
        return xt.at[u, slot_rows(rel, lo), :]

    def part(u, rel, lo, p):
        start, size = (0, 80) if p == 0 else (80, 64)
        return xt.at[u, pl.ds(pl.multiple_of((rel * 4 + lo) * SUB + start, 16), size), :]

    def gather(u, step):
        one, send = xt.at[u, pl.ds(0, SUB), :], SGATHER + u // CH
        if step in (0, 1):
            if step:
                got(u, Z, one)
            lo, p, n = (low, P0, M0) if step == 0 else (lowz, P1, M1)
            if step == 0:
                copy(u, send, Z, blk(u, HERE, low), blk(u, HERE, low), at_z)
            copy(u, send, p, blk(u, HERE, lo), blk(u, DOWN, lo), at_yp)
            copy(u, send, n, blk(u, HERE, lo), blk(u, UP, lo), at_ym)
        elif step in (2, 4):
            lo, p, far = (low, P0, F0) if step == 2 else (lowz, P1, F1)
            got(u, p, one)
            copy(u, send, far, part(u, DOWN, lo, 0), part(u, FAR, lo, 0), at_yp)
            copy(u, send, CORE, part(u, DOWN, lo, 0), part(u, FAR, lo, 0), at_yp2)
        elif step in (3, 5):
            lo, n, far = (low, M0, F0) if step == 3 else (lowz, M1, F1)
            got(u, n, one)
            copy(u, send, far, part(u, UP, lo, 1), part(u, FAR, lo, 1), at_ym)
            copy(u, send, CORE, part(u, UP, lo, 1), part(u, FAR, lo, 1), at_ym2)
        else:
            got(u, F0, one)
            got(u, F1, one)
            got(u, CORE, xt.at[u, pl.ds(0, 8 * SUB), :])

    def cross(u, step):
        lo, send = (low, lowz)[step], SGATHER + u // CH
        copy(u, send, CORE, blk(u, HERE, lo), blk(u, DOWN, lo), at_yp2)
        copy(u, send, CORE, blk(u, HERE, lo), blk(u, UP, lo), at_ym2)
        copy(u, send, CORE, blk(u, HERE, lo), blk(u, HERE, lo), at_mate)


    groups = (zf, zp, zm1, zh)

    def tproduct(u, j):
        for half in range(2):
            rows = kt[pl.ds(pl.multiple_of((groups[j] * 4 + half * 2) * SUB, 32), 2 * SUB), :]
            part = jnp.dot(rows, xt[u], preferred_element_type=F32)
            pt[u, j, pl.ds(2 * half, 2)] = part.astype(BF16).reshape(2, SUB, LN)
        s = RX + 3 * (j // 2)
        if j % 2 == 0:
            copy(u, SXT, s, pt.at[u, j, xf], xrft.at[u, j], at_xp)
            copy(u, SXT, s + 2, pt.at[u, j, xm1], xrnt.at[u, 1, j], at_xm)
        else:
            copy(u, SXT, s + 1, pt.at[u, j, xf], xrft.at[u, j], at_xm)
            copy(u, SXT, s + 2, pt.at[u, j, xp], xrnt.at[u, 0, j], at_xp)

    def trsx_mid(u, j):
        p, d = j // 2, j % 2
        to, where = (xm1, at_xm) if d else (xp, at_xp)
        got(u, RX + 3 * p + d, xrft.at[u, j])
        pt[u, j, to] = (pt[u, j, to].astype(F32) + xrft[u, j].astype(F32)).astype(BF16)
        copy(u, SXT, RX + 3 * p + 2, pt.at[u, j, to], xrnt.at[u, d, j], where)

    def trsx_fin(u, p):
        got(u, RX + 3 * p + 2, xrnt.at[u, 0])
        for j in (2 * p, 2 * p + 1):
            total = pt[u, j, x].astype(F32) + xrnt[u, 0, j].astype(F32) + xrnt[u, 1, j].astype(F32)
            s32t[u, j] = total
            zst[u, j] = total.astype(BF16)
            if j == 0:
                copy(u, SZT, RZ, zst.at[u, 0, LO, :], zrft.at[u, LO, :], at_zp)
                copy(u, SZT, RZ + 1, zst.at[u, 0, HI, :], zrft.at[u, HI, :], at_zm)
            elif j == 1:
                copy(u, SZT, RZ + 2, zst.at[u, 1, HI, :], zrnt.at[u, 0, HI, :], at_zp)
            elif j == 2:
                copy(u, SZT, RZ + 2, zst.at[u, 2, LO, :], zrnt.at[u, 1, LO, :], at_zm)

    def trsz_mid(u, p):
        j, c, where = p + 1, HI if p else LO, at_zm if p else at_zp
        got(u, RZ + p, zrft.at[u, c, :])
        zst[u, j, c, :] = (s32t[u, j, c, :] + zrft[u, c, :].astype(F32)).astype(BF16)
        copy(u, SZT, RZ + 2, zst.at[u, j, c, :], zrnt.at[u, p, c, :], where)

    def tfinish(u):
        got(u, RZ + 2, zrnt.at[u])
        total = s32t[u, 3] + zrnt[u, 0].astype(F32) + zrnt[u, 1].astype(F32)
        new = base_t[u] - RELAX * total
        xt[u + CH, slot_rows(HERE, low), :] = new.astype(BF16)
        s32t[u, 3] = total
        gather(u + CH, 0)

    def back(u):
        total = jnp.concatenate([s32t[u, 3], jnp.zeros((256 - SUB, LN), F32)], axis=0)
        wbuf[u] = total.T.reshape(16, R, 256).astype(BF16)
        for to in others:
            copy(u, SBACK, BACK, wbuf.at[u, to % 4 * 4 + to // 4], wrecv.at[u, g], {"cell": to})
        wrecv[u, g] = wbuf[u, place]

    def back_use(u):
        got(u, BACK, wrecv.at[u, pl.ds(0, 15)])
        rows = pl.ds(R * u, R)
        lam[rows, :] = base[0, rows, :]
        for q in range(16):
            start, off = window(q)
            w = wrecv[u, q].astype(F32)
            if off:
                w = pltpu.roll(w, off, axis=1)
            lam[rows, start : start + 256] = lam[rows, start : start + 256] - RELAX * w


    def turn(u):
        @pl.loop(0, WIDE // TILE)
        def _(k):
            c = pl.ds(pl.multiple_of(k * TILE, TILE), TILE)
            xm[:, c] = xt[u, c, :].T

    def cols(h):
        return pl.ds(COLS[h][0], COLS[h][1])

    def rx(to, upper):
        return pl.ds(pl.multiple_of(to * 4 * R + upper * 2 * R, 16), 2 * R)

    def product(u, h):
        v = u - CH
        start, width = COLS[h]

        wide = start + width // TILE // 2 * 2 * TILE

        @pl.loop(start // TILE, wide // TILE, step=2)
        def _(n):
            c = pl.ds(pl.multiple_of(n * TILE, TILE), 2 * TILE)
            pb[v, :, c] = jnp.dot(xm[...], kv[:, c], preferred_element_type=F32).astype(BF16)

        if wide < start + width:
            for c in (pl.ds(wide, 128), pl.ds(wide + 128, 128)):
                pb[v, :, c] = jnp.dot(xm[...], kv[:, c], preferred_element_type=F32).astype(BF16)

        s, c, lo, hi = RX + 3 * h, cols(h), pl.ds(0, 2 * R), pl.ds(2 * R, 2 * R)
        copy(u, SX, s, pb.at[v, rx(xf, 0), c], xrf.at[v, 0, :, c], at_xp)
        copy(u, SX, s + 1, pb.at[v, rx(xf, 1), c], xrf.at[v, 1, :, c], at_xm)
        copy(u, SX, s + 2, pb.at[v, rx(xp, 1), c], xrn.at[v, 0, hi, c], at_xp)
        copy(u, SX, s + 2, pb.at[v, rx(xm1, 0), c], xrn.at[v, 1, lo, c], at_xm)

    def rsx_mid(u, h, d):
        v, s, c = u - CH, RX + 3 * h, cols(h)
        got(u, s + d, xrf.at[v, d, :, c])
        r, half, where = (rx(xm1, 1), pl.ds(2 * R, 2 * R), at_xm) if d else (rx(xp, 0), pl.ds(0, 2 * R), at_xp)
        pb[v, r, c] = (pb[v, r, c].astype(F32) + xrf[v, d, :, c].astype(F32)).astype(BF16)
        copy(u, SX, s + 2, pb.at[v, r, c], xrn.at[v, d, half, c], where)

    def rsx_fin(u, h):
        v, c, s = u - CH, cols(h), RZ + 2 * h
        got(u, RX + 3 * h + 2, pb.at[v, pl.ds(0, 8 * R), c])
        r = pl.ds(pl.multiple_of(x * 4 * R, 4 * R), 4 * R)
        total = pb[v, r, c].astype(F32) + xrn[v, 0, :, c].astype(F32) + xrn[v, 1, :, c].astype(F32)
        total = total.reshape(4, R, COLS[h][1])
        s32[v, :, :, c] = total
        zs[v, :, :, c] = total.astype(BF16)
        if h == 0:
            copy(u, SZ, s, zs.at[v, zf, :, c], zrf.at[v, :, c], at_zp)
            copy(u, SZ, s + 1, zs.at[v, zm1, :, c], zrn.at[v, 1, :, c], at_zm)
        else:
            copy(u, SZ, s, zs.at[v, zf, :, c], zrf.at[v, :, c], at_zm)
            copy(u, SZ, s + 1, zs.at[v, zp, :, c], zrn.at[v, 0, :, c], at_zp)

    def rsz_mid(u, h):
        v, c, s = u - CH, cols(h), RZ + 2 * h
        to, where = (zm1, at_zm) if h else (zp, at_zp)
        got(u, s, zrf.at[v, :, c])
        zs[v, to, :, c] = (s32[v, to, :, c] + zrf[v, :, c].astype(F32)).astype(BF16)
        copy(u, SZ, s + 1, zs.at[v, to, :, c], zrn.at[v, h, :, c], where)

    def finish(u, h):
        v, c = u - CH, cols(h)
        got(u, RZ + 2 * h + 1, zrn.at[v, :, :, c])
        total = s32[v, zh, :, c] + zrn[v, 0, :, c].astype(F32) + zrn[v, 1, :, c].astype(F32)
        rows = pl.ds(R * v, R)
        out[rows, c] = base[1, rows, c] - RELAX * total


    def edge_send(it):
        state = adj if it == 0 else lam
        bsend[it, 0] = state[31:32, :]
        bsend[it, 1] = state[0:1, :]
        copy(it, SEDGE, EDGE, bsend.at[it, 0], brecv.at[it, 0], {"cell": (g + 1) % 16})
        copy(it, SEDGE, EDGE, bsend.at[it, 1], brecv.at[it, 1], {"cell": (g + 15) % 16})

    def edge_use(it):
        state = adj if it == 0 else lam
        got(it, EDGE, brecv.at[it])
        first, last = g == 0, g == 15

        @pl.loop(0, WIDE // TILE)
        def _(n):
            c = pl.ds(pl.multiple_of(n * TILE, TILE), TILE)
            now = state[:, c]
            row = lax.broadcasted_iota(jnp.int32, now.shape, 0)
            before = jnp.where(first, 0.0, brecv[it, 0, :, c])
            after = jnp.where(last, 0.0, brecv[it, 1, :, c])
            down = jnp.where(row == 0, before, pltpu.roll(now, 1, axis=0))
            up = jnp.where(row == 31, after, pltpu.roll(now, 31, axis=0))
            pick = jnp.where(sign[:, c] > 0, up, down)
            transport = speed[c][None, :] * kappa[:, :1] * (now - pick)
            base[it, :, c] = now + RELAX * (src[:, c] - transport)

    await_in(0)
    await_in(1, 2, 3)
    pack_state(2)
    pack_state(3)
    pack_state(1)
    prepare()
    pack_state(0)
    pl.semaphore_wait(barrier, 21)
    a2a(0)
    a2a(1)
    await_in(6, 7, 8, 9)
    await_in(4, 5)
    flip(4)
    a2a(2)
    edge_send(0)
    flip(5)
    flip(8)
    flip(7)
    a2a(3)
    own(0)
    gather(0, 0)
    cross(0, 0)
    own(1)
    gather(1, 0)
    flip(2)
    cross(1, 0)
    gather(0, 1)
    gather(0, 3)
    edge_use(0)
    pack_base(2)
    gather(0, 2)
    pack_base(3)
    there(3)
    gather(1, 1)
    cross(0, 1)
    own(2)
    pack_base(0)
    flip(6)
    own(3)
    pack_base(1)
    flip(0)
    gather(0, 4)
    gather(0, 5)
    gather(2, 0)
    cross(1, 1)
    gather(1, 2)
    flip(3)
    there(0)
    flip(1)
    gather(1, 4)
    gather(1, 5)
    there(2)
    there(1)
    gather(1, 3)
    gather(3, 0)
    gather(2, 1)
    gather(0, 8)
    tproduct(0, 0)
    tproduct(0, 1)
    tproduct(0, 2)
    cross(2, 1)
    tproduct(0, 3)
    gather(1, 8)
    cross(2, 0)
    gather(2, 2)
    gather(2, 3)
    tproduct(1, 0)
    tproduct(1, 1)
    gather(2, 4)
    trsx_mid(0, 0)
    gather(3, 2)
    there_use(0)
    gather(2, 5)
    gather(3, 1)
    trsx_mid(0, 1)
    gather(3, 3)
    cross(3, 1)
    tproduct(1, 2)
    trsx_mid(0, 3)
    trsx_mid(0, 2)
    cross(3, 0)
    tproduct(1, 3)
    trsx_mid(1, 0)
    trsx_mid(1, 1)
    gather(2, 8)
    tproduct(2, 0)
    trsx_fin(0, 0)
    tproduct(2, 1)
    gather(3, 5)
    gather(3, 4)
    tproduct(2, 2)
    trsx_mid(1, 2)
    trsx_mid(1, 3)
    trsx_fin(1, 0)
    tproduct(2, 3)
    trsx_mid(2, 0)
    trsx_mid(2, 1)
    trsx_fin(0, 1)
    there_use(1)
    trsz_mid(0, 1)
    gather(3, 8)
    trsz_mid(0, 0)
    tproduct(3, 0)
    tproduct(3, 1)
    trsx_mid(2, 2)
    trsx_fin(1, 1)
    tproduct(3, 2)
    trsx_mid(2, 3)
    trsz_mid(1, 0)
    trsz_mid(1, 1)
    trsx_fin(2, 0)
    tproduct(3, 3)
    tfinish(0)
    trsx_mid(3, 0)
    cross(4, 0)
    trsx_mid(3, 1)
    trsx_fin(2, 1)
    tfinish(1)
    trsx_mid(3, 3)
    trsz_mid(2, 1)
    trsz_mid(2, 0)
    gather(4, 1)
    trsx_mid(3, 2)
    there_use(2)
    there_use(3)
    gather(4, 3)
    gather(4, 2)
    cross(4, 1)
    trsx_fin(3, 0)
    gather(5, 1)
    gather(4, 4)
    gather(4, 5)
    gather(5, 3)
    trsx_fin(3, 1)
    tfinish(2)
    cross(5, 1)
    trsz_mid(3, 1)
    trsz_mid(3, 0)
    cross(5, 0)
    gather(5, 2)
    back(1)
    back(0)
    gather(5, 5)
    back(2)
    gather(5, 4)
    gather(4, 8)
    turn(4)
    gather(6, 1)
    cross(6, 0)
    product(4, 0)
    tfinish(3)
    cross(6, 1)
    back(3)
    gather(6, 3)
    product(4, 1)
    gather(5, 8)
    gather(6, 2)
    turn(5)
    gather(6, 4)
    gather(6, 5)
    product(5, 0)
    gather(7, 1)
    rsx_mid(4, 0, 0)
    cross(7, 1)
    cross(7, 0)
    rsx_mid(4, 0, 1)
    product(5, 1)
    gather(7, 3)
    gather(7, 2)
    gather(6, 8)
    turn(6)
    rsx_mid(4, 1, 0)
    back_use(1)
    gather(7, 4)
    gather(7, 5)
    rsx_mid(5, 0, 1)
    back_use(2)
    rsx_mid(5, 0, 0)
    rsx_mid(4, 1, 1)
    product(6, 0)
    rsx_fin(4, 0)
    product(6, 1)
    back_use(3)
    rsx_mid(5, 1, 1)
    rsx_mid(5, 1, 0)
    gather(7, 8)
    turn(7)
    product(7, 0)
    back_use(0)
    rsx_fin(5, 0)
    product(7, 1)
    rsx_mid(6, 0, 0)
    rsx_mid(6, 0, 1)
    rsx_mid(6, 1, 1)
    rsx_mid(6, 1, 0)
    rsx_fin(5, 1)
    rsx_mid(7, 0, 1)
    rsz_mid(4, 0)
    rsx_fin(4, 1)
    rsx_mid(7, 0, 0)
    rsx_mid(7, 1, 1)
    rsx_mid(7, 1, 0)
    rsx_fin(6, 0)
    rsx_fin(6, 1)
    rsx_fin(7, 0)
    rsx_fin(7, 1)
    rsz_mid(6, 0)
    rsz_mid(5, 1)
    rsz_mid(5, 0)
    rsz_mid(6, 1)
    rsz_mid(4, 1)
    edge_send(1)
    rsz_mid(7, 0)
    rsz_mid(7, 1)
    edge_use(1)
    finish(6, 1)
    finish(4, 1)
    finish(5, 0)
    finish(5, 1)
    finish(6, 0)
    finish(4, 0)
    finish(7, 0)
    finish(7, 1)
    gone(SALL, sbuf.at[:, pl.ds(0, 15)])
    gone(STHERE, tbuf.at[:, pl.ds(0, 15)])
    gone(SBACK, wbuf.at[:, pl.ds(0, 15)])
    for it in range(2):
        gone(SGATHER + it, xt.at[pl.ds(it * CH, CH), pl.ds(0, 15 * SUB), :])
    gone(SXT, pt.at[:, pl.ds(0, 3)])
    gone(SX, pb.at[:, pl.ds(0, 12 * R), :])
    gone(SZT, zst.at[:, pl.ds(0, 3)])
    gone(SZ, zs.at[:, pl.ds(0, 3)])
    gone(SEDGE, bsend)


def shards(adjoint, source, collision, speed, direction, labels, conductance):
    rows, width = adjoint.shape
    table = collision.reshape(-1, width)
    return pl.pallas_call(
        kernel,
        out_shape=jax.ShapeDtypeStruct((rows, width), F32),
        in_specs=[pl.BlockSpec(memory_space=pltpu.HBM)] * 7,
        out_specs=pl.BlockSpec(memory_space=pltpu.VMEM),
        scratch_shapes=[
            pltpu.VMEM(speed.shape, F32),
            pltpu.SMEM(direction.shape, jnp.int32),
            pltpu.SMEM(labels.shape, jnp.int32),
            pltpu.SMEM(conductance.shape, F32),
            pltpu.VMEM((32, WIDE), F32),
            pltpu.VMEM((32, WIDE), F32),
            pltpu.VMEM((1, WIDE), jnp.int32),
            pltpu.VMEM((32, 128), F32),
            pltpu.VMEM((WIDE, WIDE), BF16),
            pltpu.VMEM((WIDE, WIDE), BF16),
            pltpu.VMEM((32, WIDE), F32),
            pltpu.VMEM((2, 32, WIDE), F32),
            pltpu.VMEM((CH, 16, R, 256), BF16),
            pltpu.VMEM((CH, 16, R, 256), BF16),
            pltpu.VMEM((CH, 16, R, 256), BF16),
            pltpu.VMEM((CH, 16, R, 256), BF16),
            pltpu.VMEM((CH, SUB, LN), F32),
            pltpu.VMEM((CH, 16, R, 256), BF16),
            pltpu.VMEM((CH, 16, R, 256), BF16),
            pltpu.VMEM((2 * CH, WIDE, LN), BF16),
            pltpu.VMEM((LN, WIDE), BF16),
            pltpu.VMEM((CH, 4, 4, SUB, LN), BF16),
            pltpu.VMEM((CH, 4, SUB, LN), BF16),
            pltpu.VMEM((CH, 2, 4, SUB, LN), BF16),
            pltpu.VMEM((CH, 4, SUB, LN), F32),
            pltpu.VMEM((CH, 4, SUB, LN), BF16),
            pltpu.VMEM((CH, SUB, LN), BF16),
            pltpu.VMEM((CH, 2, SUB, LN), BF16),
            pltpu.VMEM((CH, LN, WIDE), BF16),
            pltpu.VMEM((CH, 2, 2 * R, WIDE), BF16),
            pltpu.VMEM((CH, 2, 4 * R, WIDE), BF16),
            pltpu.VMEM((CH, 4, R, WIDE), F32),
            pltpu.VMEM((CH, 4, R, WIDE), BF16),
            pltpu.VMEM((CH, R, WIDE), BF16),
            pltpu.VMEM((CH, 2, R, WIDE), BF16),
            pltpu.VMEM((2, 2, 1, WIDE), F32),
            pltpu.VMEM((2, 2, 1, WIDE), F32),
            pltpu.SemaphoreType.DMA((SEND,)),
            pltpu.SemaphoreType.DMA((2 * CH, RECV)),
            pltpu.SemaphoreType.DMA((10,)),
        ],
        compiler_params=pltpu.CompilerParams(collective_id=0, has_side_effects=True, vmem_limit_bytes=58 << 20),
    )(table, adjoint, source, speed, direction, labels, conductance)


def solution(mesh):
    in_specs = (
        P("cell", "mode"),
        P("cell", "mode"),
        P(None, "cell", None, "mode"),
        P("mode"),
        P("mode"),
        P("cell"),
        P(),
    )
    return jax.shard_map(shards, mesh=mesh, in_specs=in_specs, out_specs=P("cell", "mode"), check_vma=False)
```
